32 devices in a mesh: grp: 4 (over z), ex: 8 (over y, x, core).
Axes of the slice: x: 2, y: 2, z: 4, core: 2. Of those that a mesh axis runs over, the one named last changes fastest.
Arguments:
- tokens: bfloat16 [2048, 3584], P(('grp', 'ex')), may hold values from -6 to 6
- expert_ids: int32 [2048, 8], P(('grp', 'ex')), may hold values from 0 to 15, all different within a row; in each aligned block of 64 rows (0 to 63, 64 to 127, ...) at most 40 rows name the same one
- combine: float32 [2048, 8], P(('grp', 'ex')), may hold values from 0.25 to 0.5
- hot_flags: int32 [16], replicated, may hold values from 0 to 1
- gate_up_weight: bfloat16 [4, 8, 2, 3584, 512], P('grp', 'ex'), as said below
- gate_up_scale: float32 [4, 8, 2, 28, 512], P('grp', 'ex')
- down_weight: bfloat16 [4, 8, 512, 3584], P('grp', 'ex'), as said below
- down_scale: float32 [4, 8, 4, 3584], P('grp', 'ex')
Outputs:
- moe_out: bfloat16 [2048, 3584], P(('grp', 'ex'))
The draws below stay inside these ranges and needn't reach their ends.
Inputs may be any that keep to these rules, and one draw needn't show every extreme that they name: `expert_ids`: each row names 8 different experts; the 64 rows of one device name one expert at most 40 times. `gate_up_weight`: for an expert whose hot flag is 0, every entry is an integer from -8 to 7. `down_weight`: for an expert whose hot flag is 0, every entry is an integer from -8 to 7.
All inputs are finite; a program needn't handle non-finite values.
Results may differ from the reference program's by a relative error of at most 0.008.
Values may be sent and summed in bfloat16 or wider, within the bound.
A program may use at most 128 MiB of HBM per device.

```python
import math
import jax
import jax.numpy as jnp
import numpy as np
from jax import lax

D = 3584
FF = 1024
TOP = 8
GROUP = 128
TOK_DEV = 64
SLABS = 4
LANES = 8
EXPERTS = 16
FFH = 512
CAP = 40
TOKENS = 2048
N_GRP = 4
N_EX = 8


def flag_table(key):
    levels = jax.random.randint(jax.random.fold_in(key, 11), (EXPERTS,), 0, 2)
    return levels.astype(jnp.int32)


def slab_flags(key):
    flags = flag_table(key)
    pair_index = jnp.arange(SLABS, dtype=jnp.int32) // 2
    lane_index = jnp.arange(LANES, dtype=jnp.int32)
    return flags[pair_index[:, None] * LANES + lane_index[None, :]]


def mixed_weights(key, shape, fan_in, extra_dims):
    is_hot = slab_flags(key).reshape((SLABS, LANES) + (1,) * extra_dims) == 1
    real_key = jax.random.fold_in(key, 21)
    dense = jax.random.normal(real_key, shape, jnp.float32) * fan_in ** (-0.5)
    codes = jax.random.randint(jax.random.fold_in(key, 22), shape, -8, 8).astype(jnp.float32)
    return jnp.where(is_hot, dense, codes).astype(jnp.bfloat16)


def spread_scales(key, shape, fan_in):
    low_end, high_end = (math.log(0.5), math.log(2.0))
    logs = jax.random.uniform(jax.random.fold_in(key, 31), shape, jnp.float32, low_end, high_end)
    return (jnp.exp(logs) * (0.22 * fan_in ** (-0.5))).astype(jnp.float32)


def draw_hot_flags(key, part):
    return flag_table(key)


def draw_gate_up_weight(key, part):
    return mixed_weights(key, (SLABS, LANES, 2, D, FFH), D, 3)


def draw_down_weight(key, part):
    return mixed_weights(key, (SLABS, LANES, FFH, D), FF, 2)


def draw_gate_up_scale(key, part):
    return spread_scales(key, (SLABS, LANES, 2, D // GROUP, FFH), D)


def draw_down_scale(key, part):
    return spread_scales(key, (SLABS, LANES, FFH // GROUP, D), FF)


def level_of(rng, dims, cuts, low, top_value):
    factor_of = 1.0
    for position, parts in cuts:
        draws = jax.random.uniform(jax.random.fold_in(jax.random.fold_in(rng, 6), position), (parts,), jnp.float32, low / len(cuts), top_value / len(cuts))
        factor_of = factor_of * jnp.repeat(jnp.exp(draws), dims[position] // parts).reshape((-1,) + (1,) * (len(dims) - 1 - position))
    return factor_of


def routed_block(own_key, own, number, rows, number_of, top, reach, skew):
    ranking = jax.random.permutation(own_key, number_of)
    heavy_load, common = shares(number_of, rows * top, reach, skew, True), shares(number_of, rows * top, reach, skew, False)
    places = jnp.arange(number_of)

    def named(sizes, rotation):
        used = int((sizes > 0).sum())
        fixed = max(1, used // 4)
        passed = fixed + (places - fixed + rotation * (used - fixed)) % max(1, number_of - fixed)
        return jnp.zeros((number_of,), jnp.int32).at[ranking[jnp.where(places < fixed, places, passed)]].set(jnp.asarray(sizes, jnp.int32))

    sizes = jnp.where(number % 4 == 0, named(heavy_load, number // 4), named(common, number - number // 4 - 1))
    mixed = jax.random.permutation(jax.random.fold_in(own, 3), number_of)
    source_of, sink = mixed[0:number_of // 2 * 2:2], mixed[1:number_of // 2 * 2:2]
    margin = jnp.minimum(sizes[source_of] - 1, reach - sizes[sink]) // 2
    margin = jnp.where((source_of == ranking[0]) | (sink == ranking[0]) | (sizes[sink] == 0), 0, jnp.maximum(margin, 0))
    passed = jax.random.randint(jax.random.fold_in(own, 4), (number_of // 2,), 0, 1 << 20) % (margin + 1)
    sizes = sizes.at[source_of].add(-passed).at[sink].add(passed)
    labels = jnp.searchsorted(jnp.cumsum(sizes), jnp.arange(rows * top), side="right").astype(jnp.int32)
    grid = labels.reshape(top, rows).T
    grid = grid[jax.random.permutation(jax.random.fold_in(own, 1), rows)]
    rotation = jax.random.randint(jax.random.fold_in(own, 2), (rows, 1), 0, top)
    return jnp.take_along_axis(grid, (jnp.arange(top)[None, :] + rotation) % top, axis=1)


def shares(number_of, total, bound, slope, full):
    weights = [(1 << 20) // math.isqrt(rank ** slope) + 1 for rank in range(1, number_of + 1)]
    largest = bound if full else min(bound, max(-(-total // number_of), total * weights[0] // sum(weights)))
    least = 1 if total - largest >= number_of - 1 else 0
    holding, rest = [largest] + [least] * (number_of - 1), total - largest - least * (number_of - 1)
    while rest > 0:
        movable = [i for i in range(1, number_of) if holding[i] < largest] or [i for i in range(1, number_of) if holding[i] < bound]
        pool, remaining = sum([weights[i] for i in movable]), rest
        for i in movable:
            more = min(bound - holding[i], max(1, remaining * weights[i] // pool), rest)
            holding[i] = holding[i] + more
            rest = rest - more
    return np.array(holding)


def normal_values(stream_key, dims, scale, reach, shards=(), kind=jnp.bfloat16):
    factor_of = level_of(stream_key, dims, shards, -0.22, 0.18) if shards else 1.0
    array = jax.random.normal(stream_key, dims, jnp.float32) * scale * factor_of
    return jnp.minimum(jnp.maximum(array, -reach), reach).astype(kind)


def setup_inputs(seed: int = 0) -> dict:
    key_list = jax.random.split(jax.random.key(seed), 9)
    tokens = normal_values(key_list[0], (TOKENS, D), 1.0, 6.0, ((0, 32),))
    expert_ids_keys = jax.random.split(jax.random.fold_in(key_list[1], 1), TOKENS // TOK_DEV)
    expert_ids_turns = jax.random.permutation(jax.random.fold_in(key_list[1], 3), TOKENS // TOK_DEV)
    expert_ids = jax.vmap(lambda own, number: routed_block(jax.random.fold_in(key_list[1], 2), own, number, TOK_DEV, EXPERTS, TOP, CAP, 2))(expert_ids_keys, expert_ids_turns).reshape((TOKENS, TOP))
    combine = jnp.clip(0.25 + 0.25 * jax.random.uniform(key_list[2], (TOKENS, TOP), jnp.float32) ** level_of(key_list[2], (TOKENS, TOP), ((0, 32),), -0.2, 0.2), 0.25, 0.5)
    hot_flags = draw_hot_flags(jax.random.fold_in(key_list[8], 71), 0)
    gate_up_weight = draw_gate_up_weight(jax.random.fold_in(key_list[8], 71), 0)
    gate_up_scale = draw_gate_up_scale(jax.random.fold_in(key_list[8], 71), 0)
    down_weight = draw_down_weight(jax.random.fold_in(key_list[8], 71), 0)
    down_scale = draw_down_scale(jax.random.fold_in(key_list[8], 71), 0)
    return {"tokens": tokens, "expert_ids": expert_ids, "combine": combine, "hot_flags": hot_flags, "gate_up_weight": gate_up_weight, "gate_up_scale": gate_up_scale, "down_weight": down_weight, "down_scale": down_scale}


def scale_groups(weights, scales):
    row_count = weights.shape[0]
    group_count = scales.shape[0]
    shaped = weights.reshape(group_count, row_count // group_count, weights.shape[1])
    return (shaped * scales[:, None, :]).reshape(weights.shape)


def dequantize(weights, scales, is_hot):
    scaled = scale_groups(weights, scales).astype(jnp.bfloat16)
    return jnp.where(is_hot, weights, scaled)


def half_expert(token_rows, gate_up, gate_up_scales, down, down_scales, is_hot):
    gate_matrix = dequantize(gate_up[0], gate_up_scales[0], is_hot)
    up_matrix = dequantize(gate_up[1], gate_up_scales[1], is_hot)
    down_matrix = dequantize(down, down_scales, is_hot)
    gate_proj = jnp.dot(token_rows, gate_matrix, preferred_element_type=jnp.float32)
    up_proj = jnp.dot(token_rows, up_matrix, preferred_element_type=jnp.float32)
    hidden = (jax.nn.silu(gate_proj) * up_proj).astype(jnp.bfloat16)
    return jnp.dot(hidden, down_matrix, preferred_element_type=jnp.float32).astype(jnp.bfloat16)


def reference(tokens, expert_ids, combine, hot_flags, gate_up_weight, gate_up_scale, down_weight, down_scale):
    lane_count = N_EX
    expert_count = N_GRP * N_EX // 2
    most_rows = N_GRP * N_EX * CAP
    route_total = TOKENS * TOP
    flat_expert = expert_ids.reshape(route_total)
    flat_token = (jnp.arange(route_total, dtype=jnp.int32) // TOP).astype(jnp.int32)
    flat_weight = combine.reshape(route_total)
    padded_tokens = jnp.concatenate([tokens, jnp.zeros((1, D), tokens.dtype)], axis=0)

    def one_expert(running, expert_id):
        picked = jnp.nonzero(flat_expert == expert_id, size=most_rows, fill_value=route_total)[0].astype(jnp.int32)
        is_valid = picked < route_total
        safe_index = jnp.minimum(picked, route_total - 1).astype(jnp.int32)
        token_index = jnp.where(is_valid, flat_token[safe_index], TOKENS).astype(jnp.int32)
        weights_now = jnp.where(is_valid, flat_weight[safe_index], jnp.zeros((), flat_weight.dtype))
        token_rows = padded_tokens[token_index]
        pair_index = expert_id // lane_count
        lane_index = expert_id % lane_count
        is_hot = hot_flags[expert_id] == 1
        half_sum = jnp.zeros((most_rows, D), jnp.float32)
        for half_index in range(2):
            slab_index = 2 * pair_index + half_index
            partial_value = half_expert(token_rows, gate_up_weight[slab_index, lane_index], gate_up_scale[slab_index, lane_index], down_weight[slab_index, lane_index], down_scale[slab_index, lane_index], is_hot)
            half_sum = half_sum + partial_value.astype(jnp.float32)
        rounded = lax.optimization_barrier(half_sum.astype(jnp.bfloat16)).astype(jnp.float32)
        return running.at[token_index].add(weights_now[:, None] * rounded, mode="drop"), None

    running, unused = lax.scan(one_expert, jnp.zeros((TOKENS, D), jnp.float32), jnp.arange(expert_count, dtype=jnp.int32))
    return running.astype(jnp.bfloat16)
```

```python
import functools

import jax
import jax.numpy as jnp
from jax import lax
from jax.experimental import pallas as pl
from jax.experimental.pallas import tpu as pltpu
from jax.sharding import PartitionSpec as P


def dequantize(weights, scales, is_hot):
    group_count = scales.shape[0]
    shaped = weights.reshape(group_count, weights.shape[0] // group_count, weights.shape[1])
    scaled = (shaped * scales[:, None, :]).reshape(weights.shape).astype(jnp.bfloat16)
    return jnp.where(is_hot, weights, scaled)


def routed_shards(
    tokens, expert_ids, combine, hot_flags, gate_up_weight, gate_up_scale, down_weight, down_scale
):
    group_count = lax.axis_size("grp")
    lane_count = lax.axis_size("ex")
    pair_count = group_count // 2
    token_count = tokens.shape[0]
    model_width = tokens.shape[1]
    top_count = expert_ids.shape[1]
    expert_count = pair_count * lane_count
    route_count = token_count * top_count
    capacity = max(2, (5 * route_count + 4 * expert_count - 1) // (4 * expert_count))
    slot_count = expert_count * capacity
    flat_expert = expert_ids.reshape(route_count)
    route_order = jnp.arange(route_count, dtype=jnp.int32)
    earlier = (flat_expert[None, :] == flat_expert[:, None]) & (
        route_order[None, :] < route_order[:, None]
    )
    route_rank = jnp.sum(earlier, axis=1, dtype=jnp.int32)
    slot_of = flat_expert * capacity + route_rank
    slot_match = slot_of[None, :] == jnp.arange(slot_count, dtype=jnp.int32)[:, None]
    filled = jnp.any(slot_match, axis=1)
    source = jnp.sum(jnp.where(slot_match, route_order[None, :] // top_count, 0), axis=1)
    slot_rows = jnp.where(filled[:, None], tokens[source], jnp.zeros((), tokens.dtype))
    outgoing = slot_rows.reshape(pair_count, lane_count, capacity, model_width)
    own_expert = lax.axis_index("grp") // 2 * lane_count + lax.axis_index("ex")
    is_hot = hot_flags[own_expert] == 1
    gate_matrix = dequantize(gate_up_weight[0, 0, 0], gate_up_scale[0, 0, 0], is_hot)
    up_matrix = dequantize(gate_up_weight[0, 0, 1], gate_up_scale[0, 0, 1], is_hot)
    down_matrix = dequantize(down_weight[0, 0], down_scale[0, 0], is_hot)
    pair_index = flat_expert // lane_count
    lane_index = flat_expert % lane_count
    within = lax.all_to_all(outgoing, "ex", split_axis=1, concat_axis=1, tiled=True)
    doubled = jnp.repeat(within, 2, axis=0)
    arrived_block = lax.all_to_all(doubled, "grp", split_axis=0, concat_axis=0, tiled=True)
    flat_rows = arrived_block.reshape(-1, model_width)
    gate_proj = jnp.dot(flat_rows, gate_matrix, preferred_element_type=jnp.float32)
    up_proj = jnp.dot(flat_rows, up_matrix, preferred_element_type=jnp.float32)
    hidden = (jax.nn.silu(gate_proj) * up_proj).astype(jnp.bfloat16)
    partial_value = jnp.dot(hidden, down_matrix, preferred_element_type=jnp.float32).astype(
        jnp.bfloat16
    )
    across = lax.all_to_all(
        partial_value.reshape(arrived_block.shape), "grp", split_axis=0, concat_axis=0, tiled=True
    )
    returned = lax.all_to_all(across, "ex", split_axis=1, concat_axis=1, tiled=True)
    flat_back = returned.reshape(-1, model_width)
    first_index = (2 * pair_index * lane_count + lane_index) * capacity + route_rank
    second_index = first_index + lane_count * capacity
    both_halves = flat_back[first_index].astype(jnp.float32) + flat_back[second_index].astype(
        jnp.float32
    )
    expert_rows = lax.optimization_barrier(both_halves.astype(jnp.bfloat16)).astype(jnp.float32)
    weighted = expert_rows * combine.reshape(route_count)[:, None]
    return jnp.sum(weighted.reshape(token_count, top_count, model_width), axis=1).astype(
        jnp.bfloat16
    )


def column_split(width):
    blocks = width // 128
    first = max(1, blocks * 11 // 28)
    second = max(1, (blocks - 2 * first) // 2)
    last = blocks - 2 * first - second
    starts, sizes = [], []
    at = 0
    for count in (first, first, second, last):
        starts.append(at * 128)
        sizes.append(count * 128)
        at += count
    return starts, sizes


def fused_kernel(
    planes,
    experts,
    hot_ref,
    own_ref,
    ids_ref,
    combine_ref,
    gate_up_ref,
    gate_up_scale_ref,
    down_ref,
    down_scale_ref,
    out_ref,
    rows_in,
    parts,
    core_in,
    pair_in,
    last_in,
    chain_a,
    chain_b,
    pair_b,
    last_b,
    gate_up,
    down,
    hidden,
    load_sem,
    chain_a_sems,
    chain_b_sems,
    spread_sems,
    spread_b_sems,
    twin_sems,
    core_sems,
    pair_sems,
    last_sems,
    back_a_sems,
    back_b_sems,
    pair_b_sems,
    last_b_sems,
):
    f32, bf16 = jnp.float32, jnp.bfloat16
    rows, width = out_ref.shape
    units = hidden.shape[1]
    extra = rows_in.shape[-1] - width
    starts, sizes = column_split(width)
    a_size = sizes[0] + sizes[1]
    b_size = sizes[2] + sizes[3]
    a_cols = pl.ds(0, a_size)
    b_cols = pl.ds(a_size, b_size)
    b_wide = pl.ds(a_size, b_size + extra)
    cols = [pl.ds(starts[i], sizes[i]) for i in range(4)]
    wide = cols[:3] + [pl.ds(starts[3], sizes[3] + extra)]

    z = lax.axis_index("grp")
    lane = lax.axis_index("ex")
    core = lane % 2
    x = (lane // 2) % 2
    y = lane // 4
    expert = z // 2 * lax.axis_size("ex") + lane
    across_x = {"ex": lane + 2 - 4 * x}
    across_y = {"ex": lane + 4 - 8 * y}
    twin = {"ex": lane + 1 - 2 * core}
    is_hot = hot_ref[expert] == 1
    own = pl.ds(pl.multiple_of(core * rows, rows), rows)
    others = pl.ds(pl.multiple_of((1 - core) * rows, rows), rows)
    has_up = z < planes - 1
    has_down = z > 0
    above = {"grp": jnp.minimum(z + 1, planes - 1)}
    below = {"grp": jnp.maximum(z - 1, 0)}
    room = jnp.minimum(z, planes - 1 - z)
    sign = jnp.where(z < planes - 1 - z, -1, 1)
    is_end = room == 0

    def plane_of(k):
        if k == 0:
            return z
        near = z + (sign if k % 2 else -sign) * ((k + 1) // 2)
        return jnp.where(k <= 2 * room, near, z - sign * (k - room))

    groups = [plane_of(k) for k in range(planes)]
    halves = [y, 1 - y]

    def mk(source, target, send_sem, recv_sem, device):
        return pltpu.make_async_remote_copy(
            src_ref=source,
            dst_ref=target,
            send_sem=send_sem,
            recv_sem=recv_sem,
            device_id=device,
            device_id_type=pl.DeviceIdType.MESH,
        )

    finals = []
    arrived = set()
    copies = {}

    def send(key, source, target, sems, index, device):
        copy = mk(source, target, sems.at[(0,) + index], sems.at[(1,) + index], device)
        copy.start()
        copies[key] = copy
        finals.append((None, copy))

    def send_if(condition, source, target, send_sem, recv_sem, device):
        copy = mk(source, target, send_sem, recv_sem, device)

        @pl.when(condition)
        def _():
            copy.start()

        finals.append((condition, copy))

    def arrive(key):
        if key not in arrived:
            arrived.add(key)
            copies[key].wait_recv()

    barrier = pltpu.get_barrier_semaphore()
    for neighbour in (across_x, across_y, twin):
        pl.semaphore_signal(
            barrier, inc=1, device_id=neighbour, device_id_type=pl.DeviceIdType.MESH
        )
    for condition, neighbour in ((has_up, above), (has_down, below)):

        @pl.when(condition)
        def _(neighbour=neighbour):
            pl.semaphore_signal(
                barrier, inc=1, device_id=neighbour, device_id_type=pl.DeviceIdType.MESH
            )

    own_copy = pltpu.make_async_copy(
        own_ref, rows_in.at[z, y, x, own, pl.ds(0, width)], load_sem.at[0]
    )
    own_copy.start()
    loads = [
        pltpu.make_async_copy(gate_up_ref.at[0], gate_up.at[0], load_sem.at[1]),
        pltpu.make_async_copy(gate_up_ref.at[1], gate_up.at[1], load_sem.at[2]),
        pltpu.make_async_copy(down_ref, down, load_sem.at[3]),
    ]
    named = lax.broadcasted_iota(jnp.int32, (extra, rows), 0)
    which = named % experts
    rest = jnp.zeros((extra, rows), f32)
    for k in range(ids_ref.shape[0]):
        rest = rest + jnp.where(ids_ref[k : k + 1, :] == which, combine_ref[k : k + 1, :], 0.0)
    piece = jnp.zeros((extra, rows), f32)
    for k in range(3):
        rounded = rest.astype(bf16).astype(f32)
        piece = jnp.where((named >= k * experts) & (named < (k + 1) * experts), rounded, piece)
        rest = rest - rounded
    piece = jnp.transpose(piece)
    rows_in[z, y, x, own, pl.ds(width, extra)] = piece.astype(bf16)
    pl.semaphore_wait(barrier, 3 + has_up.astype(jnp.int32) + has_down.astype(jnp.int32))
    own_copy.wait()
    for load in loads:
        load.start()

    def out_a_own():
        block = rows_in.at[z, y, x, own, a_cols]
        for i, (condition, device) in enumerate(((has_up, above), (has_down, below))):
            send_if(
                condition,
                block,
                block,
                chain_a_sems.at[0, i * planes],
                chain_a_sems.at[1, z],
                device,
            )

    def onward(k):
        g = groups[k]
        rising = g < z
        target = jnp.where(rising, z + 1, z - 1)
        valid = (target >= 0) & (target < planes)
        return g, valid, {"grp": jnp.clip(target, 0, planes - 1)}

    def out_a_hop(k):
        if k >= planes:
            return
        g, valid, device = onward(k)
        block = rows_in.at[g, y, x, own, a_cols]
        copy = mk(block, block, chain_a_sems.at[0, k], chain_a_sems.at[1, g], device)
        copy.wait_recv()
        send_if(valid, block, block, chain_a_sems.at[0, k], chain_a_sems.at[1, g], device)

    def out_b_own(q):
        for t in range(2):
            if q == 0:
                arrive(("b", 0, t, t))
            else:
                arrive(("b", 0, t, 1 - t))
                arrive(("b", 0, t, 2))
        block = rows_in.at[z, halves[q], :, own, b_wide]
        for i, (condition, device) in enumerate(((has_up, above), (has_down, below))):
            send_if(
                condition,
                block,
                block,
                chain_b_sems.at[0, i * planes, q],
                chain_b_sems.at[1, z, q],
                device,
            )

    def out_b_hop(k, q):
        if k >= planes:
            return
        g, valid, device = onward(k)
        block = rows_in.at[g, halves[q], :, own, b_wide]
        copy = mk(block, block, chain_b_sems.at[0, k, q], chain_b_sems.at[1, g, q], device)
        copy.wait_recv()
        send_if(valid, block, block, chain_b_sems.at[0, k, q], chain_b_sems.at[1, g, q], device)

    def spread_first(name, k):
        if k >= planes:
            return
        sems = spread_sems if name == "a" else spread_b_sems
        base = 0 if name == "a" else 2
        for j in range(2):
            for t in range(2):
                block = rows_in.at[groups[k], y, x, own, wide[base + t]]
                index = (k, t, j) if name == "a" else (t, j)
                device = across_x if (t + j) % 2 == 0 else across_y
                send((name, k, t, j), block, block, sems, index, device)

    def spread_second(name, k):
        if k >= planes:
            return
        sems = spread_sems if name == "a" else spread_b_sems
        base = 0 if name == "a" else 2
        for t in range(2):
            arrive((name, k, t, 0))
            if t == 0:
                block, device = rows_in.at[groups[k], y, 1 - x, own, wide[base]], across_y
            else:
                block, device = rows_in.at[groups[k], 1 - y, x, own, wide[base + 1]], across_x
            index = (k, t, 2) if name == "a" else (t, 2)
            send((name, k, t, 2), block, block, sems, index, device)

    def to_twin(k, q):
        if k >= planes:
            return
        for name in ("a", "b") if k == 0 else ("a",):
            for t in range(2):
                if q == 0:
                    arrive((name, k, t, t))
                else:
                    arrive((name, k, t, 1 - t))
                    arrive((name, k, t, 2))
        block = rows_in.at[groups[k], halves[q], :, own]
        send(("twin", k, q), block, block, twin_sems, (k, q), twin)

    def gate_up_phase(k, q):
        tile = min(units, 256)

        def columns_of(n, carry):
            at = pl.ds(pl.multiple_of(n * tile, tile), tile)
            block = rows_in[groups[k], halves[q], :, :, :width].reshape(hidden.shape[0], width)
            gate = jnp.dot(block, gate_up[0, :, at], preferred_element_type=f32)
            up = jnp.dot(block, gate_up[1, :, at], preferred_element_type=f32)
            hidden[:, at] = (gate / (1.0 + jnp.exp(-gate)) * up).astype(bf16)
            return carry

        lax.fori_loop(0, units // tile, columns_of, 0)

    def down_phase(k, q):
        tile = 512 if width % 512 == 0 else 128
        more = rows_in[groups[k], halves[q], :, :, width:].reshape(hidden.shape[0], -1).astype(f32)
        column = lax.broadcasted_iota(jnp.int32, more.shape, 1)
        chosen = (
            (column == expert) | (column == expert + experts) | (column == expert + 2 * experts)
        )
        weight = jnp.sum(jnp.where(chosen, more, 0.0), axis=1, keepdims=True)

        def columns_of(n, carry):
            at = pl.ds(pl.multiple_of(n * tile, tile), tile)
            value = jnp.dot(hidden[...], down[:, at], preferred_element_type=f32)
            value = jnp.where(weight != 0.0, value * weight, 0.0).astype(bf16)
            parts[groups[k], halves[q], :, :, at] = value.reshape(2, 2 * rows, tile)
            return carry

        lax.fori_loop(0, width // tile, columns_of, 0)

    step = 16

    def accumulate(items):
        def one(i, carry):
            at = pl.multiple_of(i * step, step)
            for (g, yy, xx), start, size, buffer, index, offset in items:
                target = (
                    g, yy, xx,
                    pl.ds(pl.multiple_of(core * rows + at, step), step),
                    pl.ds(start, size),
                )
                source = index + (pl.ds(at, step), pl.ds(offset, size))
                total = parts[target].astype(f32) + buffer[source].astype(f32)
                parts[target] = total.astype(bf16)
            return carry

        lax.fori_loop(0, rows // step, one, 0)

    def compute(k, q):
        arrive(("twin", k, q))
        gate_up_phase(k, q)
        down_phase(k, q)
        send(
            ("core", k, q),
            parts.at[groups[k], halves[q], :, others],
            core_in.at[k, q],
            core_sems,
            (k, q),
            twin,
        )

    def core_add(k, q):
        arrive(("core", k, q))
        accumulate(
            [((groups[k], halves[q], i), 0, width, core_in, (k, q, i), 0) for i in range(2)]
        )

    def back_pair(name, k, t):
        g = groups[k]
        c = (0 if name == "a" else 2) + t
        target = pair_in if name == "a" else pair_b
        sems = pair_sems if name == "a" else pair_b_sems
        at = pl.ds(0, sizes[c])
        index = (k, t) if name == "a" else (t,)
        source = parts.at[g, 1 - y, :, own, cols[c]] if t == 0 else parts.at[g, :, 1 - x, own, cols[c]]
        device = across_y if t == 0 else across_x
        send(("pair", name, k, t), source, target.at[index + (slice(None), slice(None), at)], sems, index, device)

    def back_last(name, k, t):
        g = groups[k]
        c = (0 if name == "a" else 2) + t
        source = pair_in if name == "a" else pair_b
        target = last_in if name == "a" else last_b
        sems = last_sems if name == "a" else last_b_sems
        at = pl.ds(0, sizes[c])
        index = (k, t) if name == "a" else (t,)
        arrive(("pair", name, k, t))
        accumulate(
            [
                ((g, y, i) if t == 0 else (g, i, x), starts[c], sizes[c], source, index + (i,), 0)
                for i in range(2)
            ]
        )
        block = parts.at[g, y, 1 - x, own, cols[c]] if t == 0 else parts.at[g, 1 - y, x, own, cols[c]]
        device = across_x if t == 0 else across_y
        send(("last", name, k, t), block, target.at[index + (slice(None), at)], sems, index, device)

    def back_fin(name, k, t):
        g = groups[k]
        c = (0 if name == "a" else 2) + t
        source = last_in if name == "a" else last_b
        index = (k, t) if name == "a" else (t,)
        arrive(("last", name, k, t))
        accumulate([((g, y, x), starts[c], sizes[c], source, index, 0)])

    def inward(k):
        g = groups[k]
        falling = g < z
        source = jnp.where(falling, z + 1, z - 1)
        target = jnp.where(falling, z - 1, z + 1)
        valid = (source >= 0) & (source < planes)
        slot = jnp.where((target == g) & falling, planes, g)
        return g, valid, {"grp": target}, slot

    always = z >= 0

    def back_a(k, condition):
        condition = always if condition is None else condition
        g, valid, device, slot = inward(k)
        pairs = []
        for t in range(2):
            part = pl.ds(starts[t], sizes[t])
            pairs.append(
                mk(
                    parts.at[g, y, x, own, cols[t]],
                    chain_a.at[slot, :, part],
                    back_a_sems.at[0, k, t],
                    back_a_sems.at[1, slot, t],
                    device,
                )
            )
            finals.append((condition, pairs[t]))

        @pl.when(condition)
        def _():
            for t in range(2):

                @pl.when(valid)
                def _(t=t):
                    block = chain_a.at[g, :, pl.ds(starts[t], sizes[t])]
                    sem = back_a_sems.at
                    mk(block, block, sem[0, k, t], sem[1, g, t], device).wait_recv()
                    accumulate([((g, y, x), starts[t], sizes[t], chain_a, (g,), starts[t])])

                pairs[t].start()

    def back_b(k, q, condition):
        condition = always if condition is None else condition
        g, valid, device, slot = inward(k)
        copy = mk(
            parts.at[g, halves[q], :, own, b_cols],
            chain_b.at[slot, q],
            back_b_sems.at[0, k, q],
            back_b_sems.at[1, slot, q],
            device,
        )
        finals.append((condition, copy))

        @pl.when(condition)
        def _():
            @pl.when(valid)
            def _():
                block = chain_b.at[g, q]
                sem = back_b_sems.at
                mk(block, block, sem[0, k, q], sem[1, g, q], device).wait_recv()
                accumulate(
                    [
                        ((g, halves[q], i), a_size, b_size, chain_b, (g, q, i), 0)
                        for i in range(2)
                    ]
                )

            copy.start()

    def own_sides():
        return ((has_down, z, below), (has_up, planes, above))

    def own_b(q):
        for condition, slot, device in own_sides():

            @pl.when(condition)
            def _(slot=slot, device=device):
                block = chain_b.at[slot, q]
                sem = back_b_sems.at
                mk(block, block, sem[0, 0, q], sem[1, slot, q], device).wait_recv()
                accumulate(
                    [
                        ((z, halves[q], i), a_size, b_size, chain_b, (slot, q, i), 0)
                        for i in range(2)
                    ]
                )

    def own_a(t):
        for condition, slot, device in own_sides():

            @pl.when(condition)
            def _(slot=slot, device=device):
                block = chain_a.at[slot, :, pl.ds(starts[t], sizes[t])]
                sem = back_a_sems.at
                mk(block, block, sem[0, 0, t], sem[1, slot, t], device).wait_recv()
                accumulate([((z, y, x), starts[t], sizes[t], chain_a, (slot,), starts[t])])

    def scale_rows(ref, scale_of, count):
        size = ref.shape[0] // count

        def one(g, carry):
            at = pl.ds(pl.multiple_of(g * size, size), size)
            scale = jnp.where(is_hot, 1.0, scale_of(g))
            ref[at] = (ref[at].astype(f32) * scale).astype(bf16)
            return carry

        lax.fori_loop(0, count, one, 0)

    def scale_gate_up(j):
        loads[1 if j else 0].wait()
        scale_rows(
            gate_up.at[j],
            lambda g: gate_up_scale_ref[g, pl.ds(j, 1), :],
            gate_up_scale_ref.shape[0],
        )

    def scale_down():
        loads[2].wait()
        scale_rows(down, lambda g: down_scale_ref[pl.ds(g, 1), :], down_scale_ref.shape[0])

    is_mid = jnp.logical_not(is_end)
    out_a_own()
    spread_first("b", 0)
    spread_second("b", 0)
    spread_first("a", 0)
    out_b_own(0)
    out_b_own(1)
    scale_gate_up(0)
    spread_second("a", 0)
    out_a_hop(1)
    spread_first("a", 1)
    scale_gate_up(1)
    to_twin(0, 0)
    to_twin(0, 1)
    spread_second("a", 1)
    out_a_hop(2)
    spread_first("a", 2)
    scale_down()
    out_b_hop(1, 0)
    compute(0, 0)
    out_b_hop(1, 1)
    spread_second("a", 2)
    to_twin(1, 0)
    out_a_hop(3)
    spread_first("a", 3)
    compute(0, 1)
    to_twin(1, 1)
    out_b_hop(2, 0)
    compute(1, 0)
    spread_second("a", 3)
    out_b_hop(2, 1)
    to_twin(2, 0)
    compute(1, 1)
    to_twin(2, 1)
    core_add(1, 0)
    back_b(1, 0, is_end)
    core_add(1, 1)
    back_b(1, 1, is_end)
    back_pair("a", 1, 0)
    back_pair("a", 1, 1)
    out_b_hop(3, 0)
    compute(2, 0)
    out_b_hop(3, 1)
    to_twin(3, 0)
    compute(2, 1)
    to_twin(3, 1)
    core_add(2, 0)
    back_b(2, 0, is_end)
    core_add(2, 1)
    back_b(2, 1, is_end)
    back_pair("a", 2, 0)
    back_pair("a", 2, 1)
    back_last("a", 1, 0)
    back_last("a", 1, 1)
    compute(3, 0)
    back_fin("a", 1, 0)
    back_fin("a", 1, 1)
    back_a(1, is_end)
    compute(3, 1)
    back_last("a", 2, 0)
    back_last("a", 2, 1)
    core_add(3, 0)
    back_b(3, 0, is_end)
    core_add(3, 1)
    back_b(3, 1, is_end)
    back_pair("a", 3, 0)
    back_pair("a", 3, 1)
    back_b(2, 0, is_mid)
    back_b(2, 1, is_mid)
    back_fin("a", 2, 0)
    back_fin("a", 2, 1)
    back_a(2, None)
    core_add(0, 0)
    core_add(0, 1)
    back_last("a", 3, 0)
    back_last("a", 3, 1)
    back_pair("a", 0, 0)
    back_pair("a", 0, 1)
    back_b(3, 0, is_mid)
    back_b(3, 1, is_mid)
    back_fin("a", 3, 0)
    back_fin("a", 3, 1)
    back_a(3, None)
    back_last("a", 0, 0)
    back_last("a", 0, 1)
    back_b(1, 0, is_mid)
    own_b(0)
    back_b(1, 1, is_mid)
    own_b(1)
    back_a(1, is_mid)
    back_pair("b", 0, 0)
    back_pair("b", 0, 1)
    back_last("b", 0, 0)
    back_last("b", 0, 1)
    back_fin("a", 0, 0)
    back_fin("a", 0, 1)
    own_a(0)
    own_a(1)
    back_fin("b", 0, 0)
    back_fin("b", 0, 1)

    def finish(i, carry):
        at = pl.ds(pl.multiple_of(i * step, step), step)
        mine = pl.ds(pl.multiple_of(core * rows + i * step, step), step)
        out_ref[at] = parts[z, y, x, mine]
        return carry

    lax.fori_loop(0, rows // step, finish, 0)
    for condition, copy in finals:
        if condition is None:
            copy.wait_send()
        else:

            @pl.when(condition)
            def _(copy=copy):
                copy.wait_send()


def dense_shards(
    tokens, expert_ids, combine, hot_flags, gate_up_weight, gate_up_scale, down_weight, down_scale
):
    planes = lax.axis_size("grp")
    lane_count = lax.axis_size("ex")
    expert_count = planes // 2 * lane_count
    rows, width = tokens.shape
    units = down_weight.shape[2]
    extra = -(-3 * expert_count // 128) * 128
    starts, sizes = column_split(width)
    a_size, b_size = sizes[0] + sizes[1], sizes[2] + sizes[3]
    bf16 = jnp.bfloat16
    dma = pltpu.SemaphoreType.DMA
    vmem = pl.BlockSpec(memory_space=pltpu.VMEM)
    return pl.pallas_call(
        functools.partial(fused_kernel, planes, expert_count),
        out_shape=jax.ShapeDtypeStruct((rows, width), bf16),
        in_specs=[
            pl.BlockSpec(memory_space=pltpu.SMEM),
            pl.BlockSpec(memory_space=pl.ANY),
            vmem,
            vmem,
            pl.BlockSpec(memory_space=pl.ANY),
            vmem,
            pl.BlockSpec(memory_space=pl.ANY),
            vmem,
        ],
        out_specs=vmem,
        scratch_shapes=[
            pltpu.VMEM((planes, 2, 2, 2 * rows, width + extra), bf16),
            pltpu.VMEM((planes, 2, 2, 2 * rows, width), bf16),
            pltpu.VMEM((planes, 2, 2, rows, width), bf16),
            pltpu.VMEM((planes, 2, 2, rows, max(sizes[:2])), bf16),
            pltpu.VMEM((planes, 2, rows, max(sizes[:2])), bf16),
            pltpu.VMEM((planes + 1, rows, a_size), bf16),
            pltpu.VMEM((planes + 1, 2, 2, rows, b_size), bf16),
            pltpu.VMEM((2, 2, rows, max(sizes[2:])), bf16),
            pltpu.VMEM((2, rows, max(sizes[2:])), bf16),
            pltpu.VMEM((2, width, units), bf16),
            pltpu.VMEM((units, width), bf16),
            pltpu.VMEM((4 * rows, units), bf16),
            dma((4,)),
            dma((2, planes + 1)),
            dma((2, planes + 1, 2)),
            dma((2, planes, 2, 3)),
            dma((2, 2, 3)),
            dma((2, planes, 2)),
            dma((2, planes, 2)),
            dma((2, planes, 2)),
            dma((2, planes, 2)),
            dma((2, planes + 1, 2)),
            dma((2, planes + 1, 2)),
            dma((2, 2)),
            dma((2, 2)),
        ],
        compiler_params=pltpu.CompilerParams(
            collective_id=0, has_side_effects=True, vmem_limit_bytes=67043328
        ),
    )(
        hot_flags,
        tokens,
        expert_ids.T,
        combine.T,
        gate_up_weight[0, 0],
        jnp.transpose(gate_up_scale[0, 0], (1, 0, 2)),
        down_weight[0, 0],
        down_scale[0, 0],
    )


def shards(tokens, expert_ids, *rest):
    group_count = lax.axis_size("grp")
    lane_count = lax.axis_size("ex")
    token_count = tokens.shape[0]
    expert_count = group_count // 2 * lane_count
    route_count = token_count * expert_ids.shape[1]
    capacity = max(2, (5 * route_count + 4 * expert_count - 1) // (4 * expert_count))
    chip_rows = group_count * lane_count // 2 * token_count
    if group_count == 2 * 2 and lane_count == 2 * 2 * 2 and 2 * expert_count * capacity >= chip_rows:
        return dense_shards(tokens, expert_ids, *rest)
    return routed_shards(tokens, expert_ids, *rest)


def solution(mesh):
    return jax.shard_map(
        shards,
        mesh=mesh,
        in_specs=(
            P(("grp", "ex"), None),
            P(("grp", "ex"), None),
            P(("grp", "ex"), None),
            P(),
            P("grp", "ex", None, None, None),
            P("grp", "ex", None, None, None),
            P("grp", "ex", None, None),
            P("grp", "ex", None, None),
        ),
        out_specs=P(("grp", "ex"), None),
        check_vma=False,
    )
```

```python
import functools

import jax
import jax.numpy as jnp
from jax import lax
from jax.experimental import pallas as pl
from jax.experimental.pallas import tpu as pltpu
from jax.sharding import PartitionSpec as P


def dequantize(weights, scales, is_hot):
    group_count = scales.shape[0]
    shaped = weights.reshape(group_count, weights.shape[0] // group_count, weights.shape[1])
    scaled = (shaped * scales[:, None, :]).reshape(weights.shape).astype(jnp.bfloat16)
    return jnp.where(is_hot, weights, scaled)


def routed_shards(
    tokens, expert_ids, combine, hot_flags, gate_up_weight, gate_up_scale, down_weight, down_scale
):
    group_count = lax.axis_size("grp")
    lane_count = lax.axis_size("ex")
    pair_count = group_count // 2
    token_count = tokens.shape[0]
    model_width = tokens.shape[1]
    top_count = expert_ids.shape[1]
    expert_count = pair_count * lane_count
    route_count = token_count * top_count
    capacity = max(2, (5 * route_count + 4 * expert_count - 1) // (4 * expert_count))
    slot_count = expert_count * capacity
    flat_expert = expert_ids.reshape(route_count)
    route_order = jnp.arange(route_count, dtype=jnp.int32)
    earlier = (flat_expert[None, :] == flat_expert[:, None]) & (
        route_order[None, :] < route_order[:, None]
    )
    route_rank = jnp.sum(earlier, axis=1, dtype=jnp.int32)
    slot_of = flat_expert * capacity + route_rank
    slot_match = slot_of[None, :] == jnp.arange(slot_count, dtype=jnp.int32)[:, None]
    filled = jnp.any(slot_match, axis=1)
    source = jnp.sum(jnp.where(slot_match, route_order[None, :] // top_count, 0), axis=1)
    slot_rows = jnp.where(filled[:, None], tokens[source], jnp.zeros((), tokens.dtype))
    outgoing = slot_rows.reshape(pair_count, lane_count, capacity, model_width)
    own_expert = lax.axis_index("grp") // 2 * lane_count + lax.axis_index("ex")
    is_hot = hot_flags[own_expert] == 1
    gate_matrix = dequantize(gate_up_weight[0, 0, 0], gate_up_scale[0, 0, 0], is_hot)
    up_matrix = dequantize(gate_up_weight[0, 0, 1], gate_up_scale[0, 0, 1], is_hot)
    down_matrix = dequantize(down_weight[0, 0], down_scale[0, 0], is_hot)
    pair_index = flat_expert // lane_count
    lane_index = flat_expert % lane_count
    within = lax.all_to_all(outgoing, "ex", split_axis=1, concat_axis=1, tiled=True)
    doubled = jnp.repeat(within, 2, axis=0)
    arrived_block = lax.all_to_all(doubled, "grp", split_axis=0, concat_axis=0, tiled=True)
    flat_rows = arrived_block.reshape(-1, model_width)
    gate_proj = jnp.dot(flat_rows, gate_matrix, preferred_element_type=jnp.float32)
    up_proj = jnp.dot(flat_rows, up_matrix, preferred_element_type=jnp.float32)
    hidden = (jax.nn.silu(gate_proj) * up_proj).astype(jnp.bfloat16)
    partial_value = jnp.dot(hidden, down_matrix, preferred_element_type=jnp.float32).astype(
        jnp.bfloat16
    )
    across = lax.all_to_all(
        partial_value.reshape(arrived_block.shape), "grp", split_axis=0, concat_axis=0, tiled=True
    )
    returned = lax.all_to_all(across, "ex", split_axis=1, concat_axis=1, tiled=True)
    flat_back = returned.reshape(-1, model_width)
    first_index = (2 * pair_index * lane_count + lane_index) * capacity + route_rank
    second_index = first_index + lane_count * capacity
    both_halves = flat_back[first_index].astype(jnp.float32) + flat_back[second_index].astype(
        jnp.float32
    )
    expert_rows = lax.optimization_barrier(both_halves.astype(jnp.bfloat16)).astype(jnp.float32)
    weighted = expert_rows * combine.reshape(route_count)[:, None]
    return jnp.sum(weighted.reshape(token_count, top_count, model_width), axis=1).astype(
        jnp.bfloat16
    )


def column_split(width):
    blocks = width // 128
    first = max(1, blocks * 11 // 28)
    second = max(1, (blocks - 2 * first) // 2)
    last = blocks - 2 * first - second
    starts, sizes = [], []
    at = 0
    for count in (first, first, second, last):
        starts.append(at * 128)
        sizes.append(count * 128)
        at += count
    return starts, sizes


def fused_kernel(
    planes,
    experts,
    hot_ref,
    own_ref,
    ids_ref,
    combine_ref,
    gate_up_ref,
    gate_up_scale_ref,
    down_ref,
    down_scale_ref,
    out_ref,
    rows_in,
    parts,
    core_in,
    pair_in,
    last_in,
    chain_a,
    chain_b,
    pair_b,
    last_b,
    gate_up,
    down,
    hidden,
    load_sem,
    chain_a_sems,
    chain_b_sems,
    spread_sems,
    spread_b_sems,
    twin_sems,
    core_sems,
    pair_sems,
    last_sems,
    back_a_sems,
    back_b_sems,
    pair_b_sems,
    last_b_sems,
):
    f32, bf16 = jnp.float32, jnp.bfloat16
    rows, width = out_ref.shape
    units = hidden.shape[1]
    extra = rows_in.shape[-1] - width
    starts, sizes = column_split(width)
    a_size = sizes[0] + sizes[1]
    b_size = sizes[2] + sizes[3]
    b_cols = pl.ds(a_size, b_size)
    b_wide = pl.ds(a_size, b_size + extra)
    cols = [pl.ds(starts[i], sizes[i]) for i in range(4)]
    wide = cols[:3] + [pl.ds(starts[3], sizes[3] + extra)]

    z = lax.axis_index("grp")
    lane = lax.axis_index("ex")
    core = lane % 2
    x = (lane // 2) % 2
    y = lane // 4
    expert = z // 2 * lax.axis_size("ex") + lane
    across_x = {"ex": lane + 2 - 4 * x}
    across_y = {"ex": lane + 4 - 8 * y}
    twin = {"ex": lane + 1 - 2 * core}
    is_hot = hot_ref[expert] == 1
    own = pl.ds(pl.multiple_of(core * rows, rows), rows)
    others = pl.ds(pl.multiple_of((1 - core) * rows, rows), rows)
    has_up = z < planes - 1
    has_down = z > 0
    above = {"grp": jnp.minimum(z + 1, planes - 1)}
    below = {"grp": jnp.maximum(z - 1, 0)}
    room = jnp.minimum(z, planes - 1 - z)
    sign = jnp.where(z < planes - 1 - z, -1, 1)
    is_end = room == 0
    is_mid = room != 0

    def plane_of(k):
        if k == 0:
            return z
        near = z + (sign if k % 2 else -sign) * ((k + 1) // 2)
        return jnp.where(k <= 2 * room, near, z - sign * (k - room))

    groups = [plane_of(k) for k in range(planes)]
    other_x, other_y = 1 - x, 1 - y
    halves = [y, other_y]

    def mk(source, target, send_sem, recv_sem, device):
        return pltpu.make_async_remote_copy(
            src_ref=source,
            dst_ref=target,
            send_sem=send_sem,
            recv_sem=recv_sem,
            device_id=device,
            device_id_type=pl.DeviceIdType.MESH,
        )

    finals = []
    copies = {}

    def send(key, source, target, sems, index, device):
        def copy():
            return mk(source(), target(), sems.at[(0,) + index], sems.at[(1,) + index], device)

        copy().start()
        if key not in copies:
            copies[key] = copy
            finals.append((None, copy))

    def send_if(key, condition, copy):
        @pl.when(condition)
        def _():
            copy().start()

        if key not in copies:
            copies[key] = copy
            finals.append((condition, copy))

    def arrive(key):
        if key not in arrived:
            arrived.add(key)
            copies[key]().wait_recv()

    def needed(name, k, q):
        if q == 0:
            return [(name, k, t, t) for t in range(2)]
        return [(name, k, t, j) for t in range(2) for j in (1 - t, 2)]

    barrier = pltpu.get_barrier_semaphore()
    for neighbour in (across_x, across_y, twin):
        pl.semaphore_signal(
            barrier, inc=1, device_id=neighbour, device_id_type=pl.DeviceIdType.MESH
        )
    for condition, neighbour in ((has_up, above), (has_down, below)):

        @pl.when(condition)
        def _(neighbour=neighbour):
            pl.semaphore_signal(
                barrier, inc=1, device_id=neighbour, device_id_type=pl.DeviceIdType.MESH
            )

    own_copy = pltpu.make_async_copy(
        own_ref, rows_in.at[z, y, x, own, pl.ds(0, width)], load_sem.at[0]
    )
    own_copy.start()
    loads = [
        pltpu.make_async_copy(gate_up_ref.at[0], gate_up.at[0], load_sem.at[1]),
        pltpu.make_async_copy(gate_up_ref.at[1], gate_up.at[1], load_sem.at[2]),
        pltpu.make_async_copy(down_ref, down, load_sem.at[3]),
    ]
    named = lax.broadcasted_iota(jnp.int32, (extra, rows), 0)
    which = named % experts
    rest = jnp.zeros((extra, rows), f32)
    for k in range(ids_ref.shape[0]):
        rest = rest + jnp.where(ids_ref[k : k + 1, :] == which, combine_ref[k : k + 1, :], 0.0)
    piece = jnp.zeros((extra, rows), f32)
    for k in range(3):
        rounded = rest.astype(bf16).astype(f32)
        piece = jnp.where((named >= k * experts) & (named < (k + 1) * experts), rounded, piece)
        rest = rest - rounded
    piece = jnp.transpose(piece)
    rows_in[z, y, x, own, pl.ds(width, extra)] = piece.astype(bf16)
    pl.semaphore_wait(barrier, 3 + has_up.astype(jnp.int32) + has_down.astype(jnp.int32))
    own_copy.wait()
    for load in loads:
        load.start()

    def out_a_own(t):
        for i, (condition, device) in enumerate(((has_up, above), (has_down, below))):

            def copy(i=i, device=device):
                block = rows_in.at[z, y, x, own, cols[t]]
                return mk(
                    block,
                    block,
                    chain_a_sems.at[0, i * planes, t],
                    chain_a_sems.at[1, z, t],
                    device,
                )

            send_if(("za", 0, t, i), condition, copy)

    def onward(k):
        g = groups[k]
        target = jnp.where(g < z, z + 1, z - 1)
        valid = (target >= 0) & (target < planes)
        return g, valid, {"grp": jnp.clip(target, 0, planes - 1)}

    onwards = [onward(k) for k in range(planes)]

    def out_a_hop(k, t):
        g, valid, device = onwards[k]

        def copy():
            block = rows_in.at[g, y, x, own, cols[t]]
            return mk(block, block, chain_a_sems.at[0, k, t], chain_a_sems.at[1, g, t], device)

        copy().wait_recv()
        send_if(("za", k, t), valid, copy)

    def out_b_own(q):
        for key in needed("b", 0, q):
            arrive(key)
        for i, (condition, device) in enumerate(((has_up, above), (has_down, below))):

            def copy(i=i, device=device):
                block = rows_in.at[z, halves[q], :, own, b_wide]
                return mk(
                    block,
                    block,
                    chain_b_sems.at[0, i * planes, q],
                    chain_b_sems.at[1, z, q],
                    device,
                )

            send_if(("zb", 0, q, i), condition, copy)

    def out_b_hop(k, q):
        g, valid, device = onwards[k]

        def copy():
            block = rows_in.at[g, halves[q], :, own, b_wide]
            return mk(block, block, chain_b_sems.at[0, k, q], chain_b_sems.at[1, g, q], device)

        copy().wait_recv()
        send_if(("zb", k, q), valid, copy)

    def spread(name, k, t, j):
        sems = spread_sems if name == "a" else spread_b_sems
        base = 0 if name == "a" else 2
        index = (k, t, j) if name == "a" else (t, j)
        if j == 2:
            arrive((name, k, t, 0))
            yy, xx = (y, other_x) if t == 0 else (other_y, x)
        else:
            yy, xx = y, x

        def block():
            return rows_in.at[groups[k], yy, xx, own, wide[base + t]]

        over_x = (t + j) % 2 == 0 if j < 2 else t == 1
        send((name, k, t, j), block, block, sems, index, across_x if over_x else across_y)

    def to_twin(k, q):
        for name in ("a", "b") if k == 0 else ("a",):
            for key in needed(name, k, q):
                arrive(key)

        def block():
            return rows_in.at[groups[k], halves[q], :, own]

        send(("twin", k, q), block, block, twin_sems, (k, q), twin)

    def pick(pair):
        return jnp.where(is_end, pair[0], pair[1])

    def gate(g, h):
        tile = min(units, 256)

        def columns_of(n, carry):
            at = pl.ds(pl.multiple_of(n * tile, tile), tile)
            block = rows_in[g, h, :, :, :width].reshape(hidden.shape[0], width)
            gated = jnp.dot(block, gate_up[0, :, at], preferred_element_type=f32)
            up = jnp.dot(block, gate_up[1, :, at], preferred_element_type=f32)
            hidden[:, at] = (gated / (1.0 + jnp.exp(-gated)) * up).astype(bf16)
            return carry

        lax.fori_loop(0, units // tile, columns_of, 0)

    def project(g, h):
        tile = 512 if width % 512 == 0 else 128
        more = rows_in[g, h, :, :, width:].reshape(hidden.shape[0], -1).astype(f32)
        column = lax.broadcasted_iota(jnp.int32, more.shape, 1)
        chosen = (
            (column == expert) | (column == expert + experts) | (column == expert + 2 * experts)
        )
        weight = jnp.sum(jnp.where(chosen, more, 0.0), axis=1, keepdims=True)

        def columns_of(n, carry):
            at = pl.ds(pl.multiple_of(n * tile, tile), tile)
            value = jnp.dot(hidden[...], down[:, at], preferred_element_type=f32)
            value = jnp.where(weight != 0.0, value * weight, 0.0).astype(bf16)
            parts[g, h, :, :, at] = value.reshape(2, 2 * rows, tile)
            return carry

        lax.fori_loop(0, width // tile, columns_of, 0)

    step = 16

    def accumulate(items):
        def one(i, carry):
            at = pl.multiple_of(i * step, step)
            for (g, yy, xx), start, size, buffer, index, offset in items:
                target = (
                    g, yy, xx,
                    pl.ds(pl.multiple_of(core * rows + at, step), step),
                    pl.ds(start, size),
                )
                source = index + (pl.ds(at, step), pl.ds(offset, size))
                total = parts[target].astype(f32) + buffer[source].astype(f32)
                parts[target] = total.astype(bf16)
            return carry

        lax.fori_loop(0, rows // step, one, 0)

    def to_core(k, q):
        send(
            ("core", k, q),
            lambda: parts.at[groups[k], halves[q], :, others],
            lambda: core_in.at[k, q],
            core_sems,
            (k, q),
            twin,
        )

    def core_add(k, q):
        arrive(("core", k, q))
        accumulate(
            [((groups[k], halves[q], i), 0, width, core_in, (k, q, i), 0) for i in range(2)]
        )

    def back_pair(name, k, t):
        g = groups[k]
        c = (0 if name == "a" else 2) + t
        sems = pair_sems if name == "a" else pair_b_sems
        index = (k, t) if name == "a" else (t,)

        def source():
            if t == 0:
                return parts.at[g, other_y, :, own, cols[c]]
            return parts.at[g, :, other_x, own, cols[c]]

        def target():
            ref = pair_in if name == "a" else pair_b
            return ref.at[index + (slice(None), slice(None), pl.ds(0, sizes[c]))]

        device = across_y if t == 0 else across_x
        send(("pair", name, k, t), source, target, sems, index, device)

    def back_last(name, k, t):
        g = groups[k]
        c = (0 if name == "a" else 2) + t
        sems = last_sems if name == "a" else last_b_sems
        index = (k, t) if name == "a" else (t,)
        arrive(("pair", name, k, t))
        buffer = pair_in if name == "a" else pair_b
        accumulate(
            [
                ((g, y, i) if t == 0 else (g, i, x), starts[c], sizes[c], buffer, index + (i,), 0)
                for i in range(2)
            ]
        )

        def source():
            if t == 0:
                return parts.at[g, y, other_x, own, cols[c]]
            return parts.at[g, other_y, x, own, cols[c]]

        def target():
            ref = last_in if name == "a" else last_b
            return ref.at[index + (slice(None), pl.ds(0, sizes[c]))]

        device = across_x if t == 0 else across_y
        send(("last", name, k, t), source, target, sems, index, device)

    def back_fin(name, k, t):
        c = (0 if name == "a" else 2) + t
        source = last_in if name == "a" else last_b
        index = (k, t) if name == "a" else (t,)
        arrive(("last", name, k, t))
        accumulate([((groups[k], y, x), starts[c], sizes[c], source, index, 0)])

    def inward(k):
        g = groups[k]
        falling = g < z
        source = jnp.where(falling, z + 1, z - 1)
        target = jnp.where(falling, z - 1, z + 1)
        valid = (source >= 0) & (source < planes)
        slot = jnp.where((target == g) & falling, planes, g)
        return g, valid, {"grp": jnp.clip(target, 0, planes - 1)}, slot

    inwards = [inward(k) for k in range(planes)]

    def back_a(k, t):
        g, valid, device, slot = inwards[k]

        @pl.when(valid)
        def _():
            block = chain_a.at[g, :, cols[t]]
            sem = back_a_sems.at
            mk(block, block, sem[0, k, t], sem[1, g, t], device).wait_recv()
            accumulate([((g, y, x), starts[t], sizes[t], chain_a, (g,), starts[t])])

        def copy():
            return mk(
                parts.at[g, y, x, own, cols[t]],
                chain_a.at[slot, :, cols[t]],
                back_a_sems.at[0, k, t],
                back_a_sems.at[1, slot, t],
                device,
            )

        copy().start()
        if ("ra", k, t) not in copies:
            copies["ra", k, t] = copy
            finals.append((None, copy))

    def back_b(k, q):
        g, valid, device, slot = inwards[k]

        @pl.when(valid)
        def _():
            block = chain_b.at[g, q]
            sem = back_b_sems.at
            mk(block, block, sem[0, k, q], sem[1, g, q], device).wait_recv()
            accumulate(
                [((g, halves[q], i), a_size, b_size, chain_b, (g, q, i), 0) for i in range(2)]
            )

        def copy():
            return mk(
                parts.at[g, halves[q], :, own, b_cols],
                chain_b.at[slot, q],
                back_b_sems.at[0, k, q],
                back_b_sems.at[1, slot, q],
                device,
            )

        copy().start()
        if ("rb", k, q) not in copies:
            copies["rb", k, q] = copy
            finals.append((None, copy))

    def own_sides():
        return ((has_down, z, below), (has_up, planes, above))

    def own_b(q):
        for condition, slot, device in own_sides():

            @pl.when(condition)
            def _(slot=slot, device=device):
                block = chain_b.at[slot, q]
                sem = back_b_sems.at
                mk(block, block, sem[0, 0, q], sem[1, slot, q], device).wait_recv()
                accumulate(
                    [
                        ((z, halves[q], i), a_size, b_size, chain_b, (slot, q, i), 0)
                        for i in range(2)
                    ]
                )

    def own_a(t):
        for condition, slot, device in own_sides():

            @pl.when(condition)
            def _(slot=slot, device=device):
                block = chain_a.at[slot, :, pl.ds(starts[t], sizes[t])]
                sem = back_a_sems.at
                mk(block, block, sem[0, 0, t], sem[1, slot, t], device).wait_recv()
                accumulate([((z, y, x), starts[t], sizes[t], chain_a, (slot,), starts[t])])

    def scale_rows(ref, scale_of, count):
        size = ref.shape[0] // count

        def one(g, carry):
            at = pl.ds(pl.multiple_of(g * size, size), size)
            scale = jnp.where(is_hot, 1.0, scale_of(g))
            ref[at] = (ref[at].astype(f32) * scale).astype(bf16)
            return carry

        lax.fori_loop(0, count, one, 0)

    def scale_gate_up(j):
        loads[1 if j else 0].wait()
        scale_rows(
            gate_up.at[j],
            lambda g: gate_up_scale_ref[g, pl.ds(j, 1), :],
            gate_up_scale_ref.shape[0],
        )

    def scale_down():
        loads[2].wait()
        scale_rows(down, lambda g: down_scale_ref[pl.ds(g, 1), :], down_scale_ref.shape[0])

    came = [set(), set()]

    arrived = came[0]

    @pl.when(is_end)
    def _():
        spread("b", 0, 1, 0)
        spread("a", 0, 1, 0)
        spread("b", 0, 0, 0)
        out_a_own(1)
        spread("b", 0, 1, 1)
        spread("a", 0, 1, 1)
        spread("a", 0, 0, 0)
        out_a_hop(1, 1)
        spread("a", 1, 1, 0)
        out_a_own(0)
        out_b_own(0)
        out_a_hop(1, 0)
        spread("a", 1, 0, 0)
        spread("a", 0, 0, 1)
        spread("b", 0, 0, 1)
        spread("a", 1, 0, 1)
        spread("b", 0, 1, 2)
        spread("a", 1, 1, 2)
        spread("b", 0, 0, 2)
        out_a_hop(2, 0)
        spread("a", 2, 0, 0)
        out_a_hop(2, 1)
        spread("a", 1, 0, 2)
        spread("a", 2, 1, 0)
        spread("a", 0, 0, 2)
        scale_down()
        scale_gate_up(0)
        spread("a", 1, 1, 1)
        out_b_hop(1, 1)
        out_b_own(1)
        spread("a", 2, 1, 1)
        out_b_hop(1, 0)
        to_twin(1, 1)
        spread("a", 2, 1, 2)
        spread("a", 2, 0, 2)
        scale_gate_up(1)
        arrive(("twin", 1, 1))

    arrived = came[1]

    @pl.when(is_mid)
    def _():
        spread("a", 0, 0, 0)
        out_a_own(1)
        spread("b", 0, 1, 1)
        spread("b", 0, 0, 0)
        out_a_own(0)
        spread("a", 0, 1, 0)
        spread("b", 0, 1, 0)
        scale_down()
        spread("b", 0, 0, 1)
        spread("a", 0, 1, 1)
        scale_gate_up(0)
        out_a_hop(1, 1)
        out_a_hop(2, 1)
        spread("b", 0, 0, 2)
        spread("a", 0, 0, 1)
        spread("b", 0, 1, 2)
        out_a_hop(2, 0)
        spread("a", 1, 1, 1)
        out_a_hop(1, 0)
        spread("a", 0, 1, 2)
        scale_gate_up(1)
        spread("a", 0, 0, 2)
        spread("a", 2, 1, 0)
        spread("a", 1, 1, 0)
        spread("a", 1, 0, 0)
        out_b_own(0)
        spread("a", 2, 0, 0)
        spread("a", 2, 1, 1)
        out_b_own(1)
        to_twin(0, 0)
        arrive(("twin", 0, 0))

    at_group = pick((groups[1], groups[0]))
    at_half = pick((halves[1], halves[0]))
    gate(at_group, at_half)

    arrived = came[0]

    @pl.when(is_end)
    def _():
        spread("a", 2, 0, 1)
        out_a_hop(3, 1)
        to_twin(1, 0)
    project(at_group, at_half)

    arrived = came[0]

    @pl.when(is_end)
    def _():
        to_core(1, 1)
        out_a_hop(3, 0)
        spread("a", 3, 1, 0)
        spread("a", 3, 0, 0)
        arrive(("twin", 1, 0))

    arrived = came[1]

    @pl.when(is_mid)
    def _():
        to_core(0, 0)
        out_a_hop(3, 1)
        out_b_hop(1, 0)
        out_a_hop(3, 0)
        spread("a", 3, 1, 0)
        to_twin(0, 1)
        spread("a", 1, 0, 2)
        to_twin(1, 0)
        spread("a", 2, 0, 1)
        out_b_hop(2, 1)
        arrive(("twin", 0, 1))

    at_group = pick((groups[1], groups[0]))
    at_half = pick((halves[0], halves[1]))
    gate(at_group, at_half)

    arrived = came[0]

    @pl.when(is_end)
    def _():
        out_b_hop(2, 1)
        to_twin(2, 1)
        spread("a", 0, 1, 2)
        spread("a", 3, 1, 1)

    arrived = came[1]

    @pl.when(is_mid)
    def _():
        spread("a", 3, 0, 0)
        out_b_hop(2, 0)
        spread("a", 2, 1, 2)
        spread("a", 2, 0, 2)
    project(at_group, at_half)

    arrived = came[0]

    @pl.when(is_end)
    def _():
        to_core(1, 0)
        spread("a", 3, 0, 1)
        core_add(1, 1)
        spread("a", 3, 0, 2)
        arrive(("twin", 2, 1))

    arrived = came[1]

    @pl.when(is_mid)
    def _():
        to_core(0, 1)
        out_b_hop(3, 0)
        spread("a", 1, 1, 2)
        spread("a", 1, 0, 1)
        spread("a", 3, 0, 1)
        arrive(("twin", 1, 0))

    at_group = pick((groups[2], groups[1]))
    at_half = pick((halves[1], halves[0]))
    gate(at_group, at_half)

    arrived = came[0]

    @pl.when(is_end)
    def _():
        spread("a", 3, 1, 2)
        out_b_hop(2, 0)
        core_add(1, 0)
        to_twin(2, 0)
        back_pair("a", 1, 0)

    arrived = came[1]

    @pl.when(is_mid)
    def _():
        spread("a", 3, 1, 2)
        to_twin(2, 0)
        out_b_hop(1, 1)
    project(at_group, at_half)

    arrived = came[0]

    @pl.when(is_end)
    def _():
        to_core(2, 1)
        back_pair("a", 1, 1)
        arrive(("twin", 2, 0))

    arrived = came[1]

    @pl.when(is_mid)
    def _():
        to_core(1, 0)
        arrive(("twin", 2, 0))

    at_group = pick((groups[2], groups[2]))
    at_half = pick((halves[0], halves[0]))
    gate(at_group, at_half)

    arrived = came[0]

    @pl.when(is_end)
    def _():
        out_b_hop(3, 0)
        back_b(1, 1)
        back_b(1, 0)
        to_twin(3, 0)

    arrived = came[1]

    @pl.when(is_mid)
    def _():
        core_add(0, 1)
        out_b_hop(3, 1)
        to_twin(2, 1)
    project(at_group, at_half)

    arrived = came[0]

    @pl.when(is_end)
    def _():
        to_core(2, 0)
        core_add(2, 1)
        out_b_hop(3, 1)
        back_pair("a", 2, 0)
        to_twin(3, 1)
        arrive(("twin", 3, 0))

    arrived = came[1]

    @pl.when(is_mid)
    def _():
        to_core(2, 0)
        spread("a", 3, 1, 1)
        spread("a", 3, 0, 2)
        arrive(("twin", 2, 1))

    at_group = pick((groups[3], groups[2]))
    at_half = pick((halves[0], halves[1]))
    gate(at_group, at_half)

    arrived = came[0]

    @pl.when(is_end)
    def _():
        core_add(2, 0)
        back_pair("a", 2, 1)

    arrived = came[1]

    @pl.when(is_mid)
    def _():
        to_twin(1, 1)
        core_add(0, 0)
        back_pair("a", 0, 0)
        core_add(1, 0)
        back_pair("a", 0, 1)
    project(at_group, at_half)

    arrived = came[0]

    @pl.when(is_end)
    def _():
        to_core(3, 0)
        back_b(2, 0)
        arrive(("twin", 3, 1))

    arrived = came[1]

    @pl.when(is_mid)
    def _():
        to_core(2, 1)
        core_add(2, 1)
        to_twin(3, 1)
        core_add(2, 0)
        back_pair("a", 2, 0)
        arrive(("twin", 1, 1))

    at_group = pick((groups[3], groups[1]))
    at_half = pick((halves[1], halves[1]))
    gate(at_group, at_half)

    arrived = came[0]

    @pl.when(is_end)
    def _():
        to_twin(0, 1)
        back_b(2, 1)

    arrived = came[1]

    @pl.when(is_mid)
    def _():
        back_pair("a", 2, 1)
        to_twin(3, 0)
    project(at_group, at_half)

    arrived = came[0]

    @pl.when(is_end)
    def _():
        to_core(3, 1)
        core_add(3, 0)
        to_twin(0, 0)
        back_last("a", 1, 1)
        back_b(3, 0)
        back_last("a", 2, 0)
        core_add(3, 1)
        back_pair("a", 3, 0)
        back_pair("a", 3, 1)
        arrive(("twin", 0, 1))

    arrived = came[1]

    @pl.when(is_mid)
    def _():
        to_core(1, 1)
        arrive(("twin", 3, 0))

    at_group = pick((groups[0], groups[3]))
    at_half = pick((halves[1], halves[0]))
    gate(at_group, at_half)

    arrived = came[0]

    @pl.when(is_end)
    def _():
        back_last("a", 2, 1)

    arrived = came[1]

    @pl.when(is_mid)
    def _():
        core_add(1, 1)
        back_pair("a", 1, 1)
    project(at_group, at_half)

    arrived = came[0]

    @pl.when(is_end)
    def _():
        to_core(0, 1)
        back_fin("a", 2, 0)
        back_b(3, 1)
        arrive(("twin", 0, 0))

    arrived = came[1]

    @pl.when(is_mid)
    def _():
        to_core(3, 0)
        back_b(2, 0)
        back_pair("a", 1, 0)
        arrive(("twin", 3, 1))

    at_group = pick((groups[0], groups[3]))
    at_half = pick((halves[0], halves[1]))
    gate(at_group, at_half)
    project(at_group, at_half)

    arrived = came[0]

    @pl.when(is_end)
    def _():
        to_core(0, 0)
        back_last("a", 3, 0)
        back_a(2, 0)
        back_fin("a", 1, 1)
        back_last("a", 3, 1)
        back_last("a", 1, 0)
        core_add(0, 1)
        back_fin("a", 3, 0)
        back_a(3, 0)
        back_fin("a", 3, 1)
        back_a(3, 1)
        back_pair("a", 0, 0)
        back_fin("a", 2, 1)
        back_fin("a", 1, 0)
        back_a(2, 1)
        back_a(1, 1)
        core_add(0, 0)
        back_pair("a", 0, 1)
        own_b(1)
        own_b(0)
        back_pair("b", 0, 1)
        back_a(1, 0)
        back_pair("b", 0, 0)
        back_last("a", 0, 0)
        back_last("b", 0, 0)
        back_last("a", 0, 1)
        back_last("b", 0, 1)
        back_fin("b", 0, 1)
        back_fin("b", 0, 0)
        back_fin("a", 0, 0)
        own_a(0)
        back_fin("a", 0, 1)
        own_a(1)

    arrived = came[1]

    @pl.when(is_mid)
    def _():
        to_core(3, 1)
        core_add(3, 1)
        back_b(2, 1)
        back_last("a", 2, 0)
        core_add(3, 0)
        back_pair("a", 3, 0)
        back_last("a", 1, 1)
        back_b(3, 0)
        back_pair("a", 3, 1)
        back_b(3, 1)
        back_b(1, 0)
        back_fin("a", 2, 0)
        back_last("a", 3, 0)
        back_last("a", 1, 0)
        back_a(2, 0)
        back_last("a", 3, 1)
        back_last("a", 2, 1)
        own_b(1)
        own_b(0)
        back_b(1, 1)
        back_pair("b", 0, 0)
        back_fin("a", 1, 1)
        back_last("a", 0, 1)
        back_pair("b", 0, 1)
        back_fin("a", 3, 0)
        back_a(3, 0)
        back_fin("a", 3, 1)
        back_a(3, 1)
        back_fin("a", 1, 0)
        back_a(1, 0)
        back_fin("a", 2, 1)
        back_last("a", 0, 0)
        back_last("b", 0, 0)
        back_a(2, 1)
        back_last("b", 0, 1)
        back_a(1, 1)
        back_fin("a", 0, 1)
        back_fin("a", 0, 0)
        back_fin("b", 0, 1)
        back_fin("b", 0, 0)
        own_a(1)
        own_a(0)

    def finish(i, carry):
        at = pl.ds(pl.multiple_of(i * step, step), step)
        mine = pl.ds(pl.multiple_of(core * rows + i * step, step), step)
        out_ref[at] = parts[z, y, x, mine]
        return carry

    lax.fori_loop(0, rows // step, finish, 0)
    for condition, copy in finals:
        if condition is None:
            copy().wait_send()
        else:

            @pl.when(condition)
            def _(copy=copy):
                copy().wait_send()


def dense_shards(
    tokens, expert_ids, combine, hot_flags, gate_up_weight, gate_up_scale, down_weight, down_scale
):
    planes = lax.axis_size("grp")
    lane_count = lax.axis_size("ex")
    expert_count = planes // 2 * lane_count
    rows, width = tokens.shape
    units = down_weight.shape[2]
    extra = -(-3 * expert_count // 128) * 128
    starts, sizes = column_split(width)
    a_size, b_size = sizes[0] + sizes[1], sizes[2] + sizes[3]
    bf16 = jnp.bfloat16
    dma = pltpu.SemaphoreType.DMA
    vmem = pl.BlockSpec(memory_space=pltpu.VMEM)
    return pl.pallas_call(
        functools.partial(fused_kernel, planes, expert_count),
        out_shape=jax.ShapeDtypeStruct((rows, width), bf16),
        in_specs=[
            pl.BlockSpec(memory_space=pltpu.SMEM),
            pl.BlockSpec(memory_space=pl.ANY),
            vmem,
            vmem,
            pl.BlockSpec(memory_space=pl.ANY),
            vmem,
            pl.BlockSpec(memory_space=pl.ANY),
            vmem,
        ],
        out_specs=vmem,
        scratch_shapes=[
            pltpu.VMEM((planes, 2, 2, 2 * rows, width + extra), bf16),
            pltpu.VMEM((planes, 2, 2, 2 * rows, width), bf16),
            pltpu.VMEM((planes, 2, 2, rows, width), bf16),
            pltpu.VMEM((planes, 2, 2, rows, max(sizes[:2])), bf16),
            pltpu.VMEM((planes, 2, rows, max(sizes[:2])), bf16),
            pltpu.VMEM((planes + 1, rows, a_size), bf16),
            pltpu.VMEM((planes + 1, 2, 2, rows, b_size), bf16),
            pltpu.VMEM((2, 2, rows, max(sizes[2:])), bf16),
            pltpu.VMEM((2, rows, max(sizes[2:])), bf16),
            pltpu.VMEM((2, width, units), bf16),
            pltpu.VMEM((units, width), bf16),
            pltpu.VMEM((4 * rows, units), bf16),
            dma((4,)),
            dma((2, planes + 1, 2)),
            dma((2, planes + 1, 2)),
            dma((2, planes, 2, 3)),
            dma((2, 2, 3)),
            dma((2, planes, 2)),
            dma((2, planes, 2)),
            dma((2, planes, 2)),
            dma((2, planes, 2)),
            dma((2, planes + 1, 2)),
            dma((2, planes + 1, 2)),
            dma((2, 2)),
            dma((2, 2)),
        ],
        compiler_params=pltpu.CompilerParams(
            collective_id=0, has_side_effects=True, vmem_limit_bytes=67043328
        ),
    )(
        hot_flags,
        tokens,
        expert_ids.T,
        combine.T,
        gate_up_weight[0, 0],
        jnp.transpose(gate_up_scale[0, 0], (1, 0, 2)),
        down_weight[0, 0],
        down_scale[0, 0],
    )


def shards(tokens, expert_ids, *rest):
    group_count = lax.axis_size("grp")
    lane_count = lax.axis_size("ex")
    token_count = tokens.shape[0]
    expert_count = group_count // 2 * lane_count
    route_count = token_count * expert_ids.shape[1]
    capacity = max(2, (5 * route_count + 4 * expert_count - 1) // (4 * expert_count))
    chip_rows = group_count * lane_count // 2 * token_count
    if group_count == 2 * 2 and lane_count == 2 * 2 * 2 and 2 * expert_count * capacity >= chip_rows:
        return dense_shards(tokens, expert_ids, *rest)
    return routed_shards(tokens, expert_ids, *rest)


def solution(mesh):
    return jax.shard_map(
        shards,
        mesh=mesh,
        in_specs=(
            P(("grp", "ex"), None),
            P(("grp", "ex"), None),
            P(("grp", "ex"), None),
            P(),
            P("grp", "ex", None, None, None),
            P("grp", "ex", None, None, None),
            P("grp", "ex", None, None),
            P("grp", "ex", None, None),
        ),
        out_specs=P(("grp", "ex"), None),
        check_vma=False,
    )
```

```python
import functools

import jax
import jax.numpy as jnp
from jax import lax
from jax.experimental import pallas as pl
from jax.experimental.pallas import tpu as pltpu
from jax.sharding import PartitionSpec as P


def dequantize(weights, scales, is_hot):
    group_count = scales.shape[0]
    shaped = weights.reshape(group_count, weights.shape[0] // group_count, weights.shape[1])
    scaled = (shaped * scales[:, None, :]).reshape(weights.shape).astype(jnp.bfloat16)
    return jnp.where(is_hot, weights, scaled)


def routed_shards(
    tokens, expert_ids, combine, hot_flags, gate_up_weight, gate_up_scale, down_weight, down_scale
):
    group_count = lax.axis_size("grp")
    lane_count = lax.axis_size("ex")
    pair_count = group_count // 2
    token_count = tokens.shape[0]
    model_width = tokens.shape[1]
    top_count = expert_ids.shape[1]
    expert_count = pair_count * lane_count
    route_count = token_count * top_count
    capacity = max(2, (5 * route_count + 4 * expert_count - 1) // (4 * expert_count))
    slot_count = expert_count * capacity
    flat_expert = expert_ids.reshape(route_count)
    route_order = jnp.arange(route_count, dtype=jnp.int32)
    earlier = (flat_expert[None, :] == flat_expert[:, None]) & (
        route_order[None, :] < route_order[:, None]
    )
    route_rank = jnp.sum(earlier, axis=1, dtype=jnp.int32)
    slot_of = flat_expert * capacity + route_rank
    slot_match = slot_of[None, :] == jnp.arange(slot_count, dtype=jnp.int32)[:, None]
    filled = jnp.any(slot_match, axis=1)
    source = jnp.sum(jnp.where(slot_match, route_order[None, :] // top_count, 0), axis=1)
    slot_rows = jnp.where(filled[:, None], tokens[source], jnp.zeros((), tokens.dtype))
    outgoing = slot_rows.reshape(pair_count, lane_count, capacity, model_width)
    own_expert = lax.axis_index("grp") // 2 * lane_count + lax.axis_index("ex")
    is_hot = hot_flags[own_expert] == 1
    gate_matrix = dequantize(gate_up_weight[0, 0, 0], gate_up_scale[0, 0, 0], is_hot)
    up_matrix = dequantize(gate_up_weight[0, 0, 1], gate_up_scale[0, 0, 1], is_hot)
    down_matrix = dequantize(down_weight[0, 0], down_scale[0, 0], is_hot)
    pair_index = flat_expert // lane_count
    lane_index = flat_expert % lane_count
    within = lax.all_to_all(outgoing, "ex", split_axis=1, concat_axis=1, tiled=True)
    doubled = jnp.repeat(within, 2, axis=0)
    arrived_block = lax.all_to_all(doubled, "grp", split_axis=0, concat_axis=0, tiled=True)
    flat_rows = arrived_block.reshape(-1, model_width)
    gate_proj = jnp.dot(flat_rows, gate_matrix, preferred_element_type=jnp.float32)
    up_proj = jnp.dot(flat_rows, up_matrix, preferred_element_type=jnp.float32)
    hidden = (jax.nn.silu(gate_proj) * up_proj).astype(jnp.bfloat16)
    partial_value = jnp.dot(hidden, down_matrix, preferred_element_type=jnp.float32).astype(
        jnp.bfloat16
    )
    across = lax.all_to_all(
        partial_value.reshape(arrived_block.shape), "grp", split_axis=0, concat_axis=0, tiled=True
    )
    returned = lax.all_to_all(across, "ex", split_axis=1, concat_axis=1, tiled=True)
    flat_back = returned.reshape(-1, model_width)
    first_index = (2 * pair_index * lane_count + lane_index) * capacity + route_rank
    second_index = first_index + lane_count * capacity
    both_halves = flat_back[first_index].astype(jnp.float32) + flat_back[second_index].astype(
        jnp.float32
    )
    expert_rows = lax.optimization_barrier(both_halves.astype(jnp.bfloat16)).astype(jnp.float32)
    weighted = expert_rows * combine.reshape(route_count)[:, None]
    return jnp.sum(weighted.reshape(token_count, top_count, model_width), axis=1).astype(
        jnp.bfloat16
    )


def column_split(width):
    blocks = width // 128
    first = max(1, blocks * 10 // 28)
    second = max(1, (blocks - 2 * first) // 2)
    last = blocks - 2 * first - second
    starts, sizes = [], []
    at = 0
    for count in (first, first, second, last):
        starts.append(at * 128)
        sizes.append(count * 128)
        at += count
    return starts, sizes


def fused_kernel(
    planes,
    experts,
    hot_ref,
    own_ref,
    ids_ref,
    combine_ref,
    gate_up_ref,
    gate_up_scale_ref,
    down_ref,
    down_scale_ref,
    out_ref,
    rows_in,
    parts,
    core_in,
    pair_in,
    last_in,
    chain_a,
    chain_b,
    pair_b,
    last_b,
    gate_up,
    down,
    hidden,
    load_sem,
    chain_a_sems,
    chain_b_sems,
    spread_sems,
    spread_b_sems,
    twin_sems,
    core_sems,
    pair_sems,
    last_sems,
    back_a_sems,
    back_b_sems,
    pair_b_sems,
    last_b_sems,
):
    f32, bf16 = jnp.float32, jnp.bfloat16
    rows, width = out_ref.shape
    units = hidden.shape[1]
    extra = rows_in.shape[-1] - width
    starts, sizes = column_split(width)
    a_size = sizes[0] + sizes[1]
    b_size = sizes[2] + sizes[3]
    b_cols = pl.ds(a_size, b_size)
    b_wide = pl.ds(a_size, b_size + extra)
    cols = [pl.ds(starts[i], sizes[i]) for i in range(4)]
    wide = cols[:3] + [pl.ds(starts[3], sizes[3] + extra)]

    z = lax.axis_index("grp")
    lane = lax.axis_index("ex")
    core = lane % 2
    x = (lane // 2) % 2
    y = lane // 4
    expert = z // 2 * lax.axis_size("ex") + lane
    across_x = {"ex": lane + 2 - 4 * x}
    across_y = {"ex": lane + 4 - 8 * y}
    twin = {"ex": lane + 1 - 2 * core}
    is_hot = hot_ref[expert] == 1
    own = pl.ds(pl.multiple_of(core * rows, rows), rows)
    others = pl.ds(pl.multiple_of((1 - core) * rows, rows), rows)
    has_up = z < planes - 1
    has_down = z > 0
    above = {"grp": jnp.minimum(z + 1, planes - 1)}
    below = {"grp": jnp.maximum(z - 1, 0)}
    room = jnp.minimum(z, planes - 1 - z)
    sign = jnp.where(z < planes - 1 - z, -1, 1)
    is_end = room == 0
    is_mid = room != 0

    def plane_of(k):
        if k == 0:
            return z
        near = z + (sign if k % 2 else -sign) * ((k + 1) // 2)
        return jnp.where(k <= 2 * room, near, z - sign * (k - room))

    groups = [plane_of(k) for k in range(planes)]
    other_x, other_y = 1 - x, 1 - y
    halves = [y, other_y]

    def mk(source, target, send_sem, recv_sem, device):
        return pltpu.make_async_remote_copy(
            src_ref=source,
            dst_ref=target,
            send_sem=send_sem,
            recv_sem=recv_sem,
            device_id=device,
            device_id_type=pl.DeviceIdType.MESH,
        )

    finals = []
    copies = {}

    def send(key, source, target, sems, index, device):
        def copy():
            return mk(source(), target(), sems.at[(0,) + index], sems.at[(1,) + index], device)

        copy().start()
        if key not in copies:
            copies[key] = copy
            finals.append((None, copy))

    def send_if(key, condition, copy):
        @pl.when(condition)
        def _():
            copy().start()

        if key not in copies:
            copies[key] = copy
            finals.append((condition, copy))

    def arrive(key):
        if key not in arrived:
            arrived.add(key)
            copies[key]().wait_recv()

    def needed(name, k, q):
        if q == 0:
            return [(name, k, t, t) for t in range(2)]
        return [(name, k, t, j) for t in range(2) for j in (1 - t, 2)]

    barrier = pltpu.get_barrier_semaphore()
    for neighbour in (across_x, across_y, twin):
        pl.semaphore_signal(
            barrier, inc=1, device_id=neighbour, device_id_type=pl.DeviceIdType.MESH
        )
    for condition, neighbour in ((has_up, above), (has_down, below)):

        @pl.when(condition)
        def _(neighbour=neighbour):
            pl.semaphore_signal(
                barrier, inc=1, device_id=neighbour, device_id_type=pl.DeviceIdType.MESH
            )

    own_copy = pltpu.make_async_copy(
        own_ref, rows_in.at[z, y, x, own, pl.ds(0, width)], load_sem.at[0]
    )
    own_copy.start()
    loads = [
        pltpu.make_async_copy(gate_up_ref.at[0], gate_up.at[0], load_sem.at[1]),
        pltpu.make_async_copy(gate_up_ref.at[1], gate_up.at[1], load_sem.at[2]),
        pltpu.make_async_copy(down_ref, down, load_sem.at[3]),
    ]
    named = lax.broadcasted_iota(jnp.int32, (extra, rows), 0)
    which = named % experts
    rest = jnp.zeros((extra, rows), f32)
    for k in range(ids_ref.shape[0]):
        rest = rest + jnp.where(ids_ref[k : k + 1, :] == which, combine_ref[k : k + 1, :], 0.0)
    piece = jnp.zeros((extra, rows), f32)
    for k in range(3):
        rounded = rest.astype(bf16).astype(f32)
        piece = jnp.where((named >= k * experts) & (named < (k + 1) * experts), rounded, piece)
        rest = rest - rounded
    piece = jnp.transpose(piece)
    rows_in[z, y, x, own, pl.ds(width, extra)] = piece.astype(bf16)
    pl.semaphore_wait(barrier, 3 + has_up.astype(jnp.int32) + has_down.astype(jnp.int32))
    own_copy.wait()
    for load in loads:
        load.start()

    def out_a_own(t):
        for i, (condition, device) in enumerate(((has_up, above), (has_down, below))):

            def copy(i=i, device=device):
                block = rows_in.at[z, y, x, own, cols[t]]
                return mk(
                    block,
                    block,
                    chain_a_sems.at[0, i * planes, t],
                    chain_a_sems.at[1, z, t],
                    device,
                )

            send_if(("za", 0, t, i), condition, copy)

    def onward(k):
        g = groups[k]
        target = jnp.where(g < z, z + 1, z - 1)
        valid = (target >= 0) & (target < planes)
        return g, valid, {"grp": jnp.clip(target, 0, planes - 1)}

    onwards = [onward(k) for k in range(planes)]

    def out_a_hop(k, t):
        g, valid, device = onwards[k]

        def copy():
            block = rows_in.at[g, y, x, own, cols[t]]
            return mk(block, block, chain_a_sems.at[0, k, t], chain_a_sems.at[1, g, t], device)

        copy().wait_recv()
        send_if(("za", k, t), valid, copy)

    quarters = [(y, x), (y, other_x), (other_y, x), (other_y, other_x)]
    needed_b = [
        [],
        [("b", 0, 0, 0), ("b", 0, 1, 1)],
        [("b", 0, 1, 0), ("b", 0, 0, 1)],
        [("b", 0, 0, 2), ("b", 0, 1, 2)],
    ]

    def beside(side):
        target = z - sign if side else z + sign
        valid = (target >= 0) & (target < planes)
        return valid, {"grp": jnp.clip(target, 0, planes - 1)}

    besides = [beside(side) for side in range(2)]

    def out_b_own(c, side):
        for key in needed_b[c]:
            arrive(key)
        valid, device = besides[side]

        def copy():
            block = rows_in.at[z, quarters[c][0], quarters[c][1], own, b_wide]
            return mk(
                block,
                block,
                chain_b_sems.at[0, side * planes, c],
                chain_b_sems.at[1, z, c],
                device,
            )

        send_if(("zb", 0, c, side), valid, copy)

    def out_b_hop(k, c):
        g, valid, device = onwards[k]

        def copy():
            block = rows_in.at[g, quarters[c][0], quarters[c][1], own, b_wide]
            return mk(block, block, chain_b_sems.at[0, k, c], chain_b_sems.at[1, g, c], device)

        copy().wait_recv()
        send_if(("zb", k, c), valid, copy)

    def spread(name, k, t, j):
        sems = spread_sems if name == "a" else spread_b_sems
        base = 0 if name == "a" else 2
        index = (k, t, j) if name == "a" else (t, j)
        if j == 2:
            arrive((name, k, t, 0))
            yy, xx = (y, other_x) if t == 0 else (other_y, x)
        else:
            yy, xx = y, x

        def block():
            return rows_in.at[groups[k], yy, xx, own, wide[base + t]]

        over_x = (t + j) % 2 == 0 if j < 2 else t == 1
        send((name, k, t, j), block, block, sems, index, across_x if over_x else across_y)

    def to_twin(k, q):
        for name in ("a", "b") if k == 0 else ("a",):
            for key in needed(name, k, q):
                arrive(key)

        def block():
            return rows_in.at[groups[k], halves[q], :, own]

        send(("twin", k, q), block, block, twin_sems, (k, q), twin)

    def pick(pair):
        return jnp.where(is_end, pair[0], pair[1])

    def gate(g, h):
        tile = min(units, 256)

        def columns_of(n, carry):
            at = pl.ds(pl.multiple_of(n * tile, tile), tile)
            block = rows_in[g, h, :, :, :width].reshape(hidden.shape[0], width)
            gated = jnp.dot(block, gate_up[0, :, at], preferred_element_type=f32)
            up = jnp.dot(block, gate_up[1, :, at], preferred_element_type=f32)
            hidden[:, at] = (gated / (1.0 + jnp.exp(-gated)) * up).astype(bf16)
            return carry

        lax.fori_loop(0, units // tile, columns_of, 0)

    def project(g, h):
        tile = 512 if width % 512 == 0 else 128
        more = rows_in[g, h, :, :, width:].reshape(hidden.shape[0], -1).astype(f32)
        column = lax.broadcasted_iota(jnp.int32, more.shape, 1)
        chosen = (
            (column == expert) | (column == expert + experts) | (column == expert + 2 * experts)
        )
        weight = jnp.sum(jnp.where(chosen, more, 0.0), axis=1, keepdims=True)

        def columns_of(n, carry):
            at = pl.ds(pl.multiple_of(n * tile, tile), tile)
            value = jnp.dot(hidden[...], down[:, at], preferred_element_type=f32)
            value = jnp.where(weight != 0.0, value * weight, 0.0).astype(bf16)
            parts[g, h, :, :, at] = value.reshape(2, 2 * rows, tile)
            return carry

        lax.fori_loop(0, width // tile, columns_of, 0)

    step = 16

    def accumulate(items):
        def one(i, carry):
            at = pl.multiple_of(i * step, step)
            for (g, yy, xx), start, size, buffer, index, offset in items:
                target = (
                    g, yy, xx,
                    pl.ds(pl.multiple_of(core * rows + at, step), step),
                    pl.ds(start, size),
                )
                source = index + (pl.ds(at, step), pl.ds(offset, size))
                total = parts[target].astype(f32) + buffer[source].astype(f32)
                parts[target] = total.astype(bf16)
            return carry

        lax.fori_loop(0, rows // step, one, 0)

    def to_core(k, q):
        send(
            ("core", k, q),
            lambda: parts.at[groups[k], halves[q], :, others],
            lambda: core_in.at[k, q],
            core_sems,
            (k, q),
            twin,
        )

    def core_add(k, q):
        arrive(("core", k, q))
        accumulate(
            [((groups[k], halves[q], i), 0, width, core_in, (k, q, i), 0) for i in range(2)]
        )

    def back_pair(name, k, t):
        g = groups[k]
        c = (0 if name == "a" else 2) + t
        sems = pair_sems if name == "a" else pair_b_sems
        index = (k, t) if name == "a" else (t,)

        def source():
            if t == 0:
                return parts.at[g, other_y, :, own, cols[c]]
            return parts.at[g, :, other_x, own, cols[c]]

        def target():
            ref = pair_in if name == "a" else pair_b
            return ref.at[index + (slice(None), slice(None), pl.ds(0, sizes[c]))]

        device = across_y if t == 0 else across_x
        send(("pair", name, k, t), source, target, sems, index, device)

    def back_last(name, k, t):
        g = groups[k]
        c = (0 if name == "a" else 2) + t
        sems = last_sems if name == "a" else last_b_sems
        index = (k, t) if name == "a" else (t,)
        arrive(("pair", name, k, t))
        buffer = pair_in if name == "a" else pair_b
        accumulate(
            [
                ((g, y, i) if t == 0 else (g, i, x), starts[c], sizes[c], buffer, index + (i,), 0)
                for i in range(2)
            ]
        )

        def source():
            if t == 0:
                return parts.at[g, y, other_x, own, cols[c]]
            return parts.at[g, other_y, x, own, cols[c]]

        def target():
            ref = last_in if name == "a" else last_b
            return ref.at[index + (slice(None), pl.ds(0, sizes[c]))]

        device = across_x if t == 0 else across_y
        send(("last", name, k, t), source, target, sems, index, device)

    def back_fin(name, k, t):
        c = (0 if name == "a" else 2) + t
        source = last_in if name == "a" else last_b
        index = (k, t) if name == "a" else (t,)
        arrive(("last", name, k, t))
        accumulate([((groups[k], y, x), starts[c], sizes[c], source, index, 0)])

    def inward(k):
        g = groups[k]
        falling = g < z
        source = jnp.where(falling, z + 1, z - 1)
        target = jnp.where(falling, z - 1, z + 1)
        valid = (source >= 0) & (source < planes)
        slot = jnp.where((target == g) & falling, planes, g)
        return g, valid, {"grp": jnp.clip(target, 0, planes - 1)}, slot

    inwards = [inward(k) for k in range(planes)]

    def back_a(k, t):
        g, valid, device, slot = inwards[k]

        @pl.when(valid)
        def _():
            block = chain_a.at[g, :, cols[t]]
            sem = back_a_sems.at
            mk(block, block, sem[0, k, t], sem[1, g, t], device).wait_recv()
            accumulate([((g, y, x), starts[t], sizes[t], chain_a, (g,), starts[t])])

        def copy():
            return mk(
                parts.at[g, y, x, own, cols[t]],
                chain_a.at[slot, :, cols[t]],
                back_a_sems.at[0, k, t],
                back_a_sems.at[1, slot, t],
                device,
            )

        copy().start()
        if ("ra", k, t) not in copies:
            copies["ra", k, t] = copy
            finals.append((None, copy))

    def back_b(k, c):
        g, valid, device, slot = inwards[k]
        yy, xx = quarters[c]

        @pl.when(valid)
        def _():
            block = chain_b.at[g, c]
            sem = back_b_sems.at
            mk(block, block, sem[0, k, c], sem[1, g, c], device).wait_recv()
            accumulate([((g, yy, xx), a_size, b_size, chain_b, (g, c), 0)])

        def copy():
            return mk(
                parts.at[g, yy, xx, own, b_cols],
                chain_b.at[slot, c],
                back_b_sems.at[0, k, c],
                back_b_sems.at[1, slot, c],
                device,
            )

        copy().start()
        if ("rb", k, c) not in copies:
            copies["rb", k, c] = copy
            finals.append((None, copy))

    def own_sides():
        return ((has_down, z, below), (has_up, planes, above))

    def own_b(c):
        for condition, slot, device in own_sides():

            @pl.when(condition)
            def _(slot=slot, device=device):
                block = chain_b.at[slot, c]
                sem = back_b_sems.at
                mk(block, block, sem[0, 0, c], sem[1, slot, c], device).wait_recv()
                accumulate([((z, *quarters[c]), a_size, b_size, chain_b, (slot, c), 0)])

    def own_a(t):
        for condition, slot, device in own_sides():

            @pl.when(condition)
            def _(slot=slot, device=device):
                block = chain_a.at[slot, :, pl.ds(starts[t], sizes[t])]
                sem = back_a_sems.at
                mk(block, block, sem[0, 0, t], sem[1, slot, t], device).wait_recv()
                accumulate([((z, y, x), starts[t], sizes[t], chain_a, (slot,), starts[t])])

    def scale_rows(ref, scale_of, count):
        size = ref.shape[0] // count

        def one(g, carry):
            at = pl.ds(pl.multiple_of(g * size, size), size)
            scale = jnp.where(is_hot, 1.0, scale_of(g))
            ref[at] = (ref[at].astype(f32) * scale).astype(bf16)
            return carry

        lax.fori_loop(0, count, one, 0)

    def scale_gate_up(j):
        loads[1 if j else 0].wait()
        scale_rows(
            gate_up.at[j],
            lambda g: gate_up_scale_ref[g, pl.ds(j, 1), :],
            gate_up_scale_ref.shape[0],
        )

    def scale_down():
        loads[2].wait()
        scale_rows(down, lambda g: down_scale_ref[pl.ds(g, 1), :], down_scale_ref.shape[0])

    came = [set(), set()]

    arrived = came[0]

    @pl.when(is_end)
    def _():
        spread("b", 0, 0, 0)
        spread("a", 0, 1, 0)
        spread("a", 0, 1, 1)
        out_a_own(1)
        spread("b", 0, 1, 0)
        out_a_own(0)
        spread("b", 0, 1, 1)
        spread("a", 0, 0, 0)
        spread("b", 0, 0, 1)
        spread("b", 0, 1, 2)
        out_b_own(1, 1)
        spread("b", 0, 0, 2)
        scale_gate_up(1)
        spread("a", 0, 1, 2)
        out_a_hop(1, 1)
        spread("a", 0, 0, 1)
        out_a_hop(1, 0)
        out_b_own(0, 1)
        spread("a", 0, 0, 2)
        scale_gate_up(0)
        out_a_hop(2, 1)
        to_twin(0, 0)
        out_b_own(2, 1)
        out_b_own(3, 1)
        spread("a", 1, 0, 1)
        out_a_hop(2, 0)
        spread("a", 2, 0, 0)
        to_twin(0, 1)
        scale_down()
        out_a_hop(3, 1)
        spread("a", 2, 1, 0)
        spread("a", 3, 1, 1)
        arrive(("twin", 0, 0))

    arrived = came[1]

    @pl.when(is_mid)
    def _():
        out_a_own(0)
        spread("b", 0, 1, 0)
        spread("b", 0, 1, 1)
        spread("b", 0, 0, 0)
        out_a_own(1)
        scale_down()
        spread("b", 0, 1, 2)
        spread("a", 0, 1, 1)
        out_a_hop(2, 0)
        out_a_hop(1, 1)
        spread("a", 1, 1, 1)
        spread("b", 0, 0, 1)
        spread("a", 1, 1, 0)
        out_a_hop(1, 0)
        spread("a", 1, 0, 0)
        spread("a", 1, 0, 1)
        scale_gate_up(0)
        out_a_hop(2, 1)
        out_a_hop(3, 1)
        spread("a", 2, 1, 0)
        out_b_hop(1, 1)
        spread("a", 3, 1, 0)
        out_a_hop(3, 0)
        out_b_hop(1, 0)
        scale_gate_up(1)
        to_twin(1, 0)
        spread("a", 3, 0, 0)
        out_b_hop(1, 2)
        spread("a", 1, 1, 2)
        out_b_hop(3, 1)
        spread("a", 1, 0, 2)
        arrive(("twin", 1, 0))

    at_group = pick((groups[0], groups[1]))
    at_half = pick((halves[0], halves[0]))
    gate(at_group, at_half)

    arrived = came[0]

    @pl.when(is_end)
    def _():
        out_a_hop(3, 0)
        spread("a", 3, 0, 0)
        spread("a", 3, 1, 0)

    arrived = came[1]

    @pl.when(is_mid)
    def _():
        spread("a", 3, 1, 1)
        out_b_hop(1, 3)
        spread("b", 0, 0, 2)
        spread("a", 0, 1, 0)
        spread("a", 0, 0, 0)
        out_b_own(1, 1)
        out_b_own(0, 1)
        spread("a", 3, 1, 2)
        spread("a", 2, 0, 0)
        spread("a", 2, 1, 1)
        out_b_hop(3, 0)
        out_b_hop(3, 2)
        spread("a", 3, 0, 1)
        to_twin(1, 1)
    project(at_group, at_half)

    arrived = came[0]

    @pl.when(is_end)
    def _():
        to_core(0, 0)
        spread("a", 2, 1, 1)
        spread("a", 3, 0, 1)
        arrive(("twin", 0, 1))

    arrived = came[1]

    @pl.when(is_mid)
    def _():
        to_core(1, 0)
        out_b_hop(3, 3)
        out_b_own(3, 1)
        arrive(("twin", 1, 1))

    at_group = pick((groups[0], groups[1]))
    at_half = pick((halves[1], halves[1]))
    gate(at_group, at_half)

    arrived = came[0]

    @pl.when(is_end)
    def _():
        out_b_hop(3, 0)
        spread("a", 3, 1, 2)
        out_b_hop(3, 1)
        to_twin(3, 0)
        spread("a", 1, 0, 0)

    arrived = came[1]

    @pl.when(is_mid)
    def _():
        core_add(1, 0)
        out_b_hop(2, 1)
        spread("a", 3, 0, 2)
        to_twin(3, 0)
    project(at_group, at_half)

    arrived = came[0]

    @pl.when(is_end)
    def _():
        to_core(0, 1)
        spread("a", 3, 0, 2)
        spread("a", 1, 1, 1)
        arrive(("twin", 3, 0))

    arrived = came[1]

    @pl.when(is_mid)
    def _():
        to_core(1, 1)
        out_b_hop(2, 0)
        spread("a", 0, 1, 2)
        out_b_own(2, 1)
        spread("a", 2, 0, 1)
        arrive(("twin", 3, 0))

    at_group = pick((groups[3], groups[3]))
    at_half = pick((halves[0], halves[0]))
    gate(at_group, at_half)

    arrived = came[0]

    @pl.when(is_end)
    def _():
        out_b_hop(3, 2)
        spread("a", 1, 1, 0)
        out_b_hop(3, 3)
        spread("a", 2, 0, 1)
        core_add(0, 1)
        to_twin(3, 1)
        core_add(0, 0)

    arrived = came[1]

    @pl.when(is_mid)
    def _():
        spread("a", 2, 1, 2)
        spread("a", 0, 0, 1)
        out_b_hop(2, 3)
        to_twin(3, 1)
        out_b_hop(2, 2)
    project(at_group, at_half)

    arrived = came[0]

    @pl.when(is_end)
    def _():
        to_core(3, 0)
        spread("a", 2, 0, 2)
        spread("a", 2, 1, 2)
        arrive(("twin", 3, 1))

    arrived = came[1]

    @pl.when(is_mid)
    def _():
        to_core(3, 0)
        spread("a", 2, 0, 2)
        out_b_own(3, 0)
        to_twin(2, 0)
        out_b_own(2, 0)
        core_add(1, 1)
        back_pair("a", 1, 1)
        arrive(("twin", 3, 1))

    at_group = pick((groups[3], groups[3]))
    at_half = pick((halves[1], halves[1]))
    gate(at_group, at_half)

    arrived = came[0]

    @pl.when(is_end)
    def _():
        out_b_hop(2, 0)
        out_b_hop(2, 1)
        to_twin(2, 0)
        spread("a", 1, 1, 2)
        core_add(3, 0)
        spread("a", 1, 0, 2)
        back_b(3, 1)
        back_b(3, 0)

    arrived = came[1]

    @pl.when(is_mid)
    def _():
        to_twin(0, 0)
        back_pair("a", 1, 0)
    project(at_group, at_half)

    arrived = came[0]

    @pl.when(is_end)
    def _():
        to_core(3, 1)
        arrive(("twin", 2, 0))

    arrived = came[1]

    @pl.when(is_mid)
    def _():
        to_core(3, 1)
        spread("a", 0, 0, 2)
        out_b_own(1, 0)
        out_b_own(0, 0)
        arrive(("twin", 2, 0))

    at_group = pick((groups[2], groups[2]))
    at_half = pick((halves[0], halves[0]))
    gate(at_group, at_half)

    arrived = came[0]

    @pl.when(is_end)
    def _():
        core_add(3, 1)
        back_pair("a", 3, 1)
        out_b_hop(2, 2)
        out_b_hop(2, 3)
        to_twin(2, 1)
        back_pair("a", 3, 0)
        back_pair("a", 0, 1)
        back_b(3, 2)

    arrived = came[1]

    @pl.when(is_mid)
    def _():
        core_add(3, 0)
        core_add(3, 1)
    project(at_group, at_half)

    arrived = came[0]

    @pl.when(is_end)
    def _():
        to_core(2, 0)
        back_b(3, 3)
        arrive(("twin", 2, 1))

    arrived = came[1]

    @pl.when(is_mid)
    def _():
        to_core(2, 0)
        back_b(3, 1)
        to_twin(2, 1)
        back_b(3, 0)
        back_pair("a", 3, 1)
        arrive(("twin", 0, 0))

    at_group = pick((groups[2], groups[0]))
    at_half = pick((halves[1], halves[0]))
    gate(at_group, at_half)

    arrived = came[0]

    @pl.when(is_end)
    def _():
        core_add(2, 0)
        back_b(2, 1)
        out_b_hop(1, 3)

    arrived = came[1]

    @pl.when(is_mid)
    def _():
        core_add(2, 0)
        back_pair("a", 3, 0)
    project(at_group, at_half)

    arrived = came[0]

    @pl.when(is_end)
    def _():
        to_core(2, 1)
        back_last("a", 3, 1)
        out_b_hop(1, 2)
        back_b(2, 0)
        to_twin(1, 1)
        core_add(2, 1)
        back_b(2, 3)
        back_last("a", 3, 0)
        back_pair("a", 2, 0)
        out_b_hop(1, 0)
        out_b_hop(1, 1)
        back_fin("a", 3, 1)
        to_twin(1, 0)
        back_a(3, 1)
        back_pair("a", 2, 1)
        back_b(2, 2)
        arrive(("twin", 1, 1))

    arrived = came[1]

    @pl.when(is_mid)
    def _():
        to_core(0, 0)
        back_b(3, 3)
        back_last("a", 1, 0)
        back_b(3, 2)
        arrive(("twin", 2, 1))

    at_group = pick((groups[1], groups[2]))
    at_half = pick((halves[1], halves[1]))
    gate(at_group, at_half)
    project(at_group, at_half)

    arrived = came[0]

    @pl.when(is_end)
    def _():
        to_core(1, 1)
        back_pair("a", 0, 0)
        back_fin("a", 3, 0)
        back_a(3, 0)
        out_b_own(3, 0)
        out_b_own(0, 0)
        arrive(("twin", 1, 0))

    arrived = came[1]

    @pl.when(is_mid)
    def _():
        to_core(2, 1)
        to_twin(0, 1)
        back_last("a", 3, 1)
        back_last("a", 3, 0)
        back_b(1, 0)
        core_add(2, 1)
        back_pair("a", 2, 1)
        back_pair("a", 2, 0)
        back_b(1, 3)
        back_b(2, 3)
        back_b(1, 2)
        arrive(("twin", 0, 1))

    at_group = pick((groups[1], groups[0]))
    at_half = pick((halves[0], halves[1]))
    gate(at_group, at_half)

    arrived = came[0]

    @pl.when(is_end)
    def _():
        core_add(1, 1)
    project(at_group, at_half)

    arrived = came[0]

    @pl.when(is_end)
    def _():
        to_core(1, 0)
        back_b(1, 2)
        out_b_own(2, 0)
        back_last("a", 2, 0)
        back_b(1, 3)
        back_last("a", 2, 1)
        back_pair("a", 1, 0)
        core_add(1, 0)
        back_pair("a", 1, 1)
        own_b(0)
        back_b(1, 1)
        back_fin("a", 2, 0)
        own_b(2)
        own_b(1)
        back_a(2, 0)
        own_b(3)
        back_pair("b", 0, 1)
        back_last("a", 1, 1)
        back_b(1, 0)
        back_fin("a", 2, 1)
        back_last("a", 1, 0)
        back_last("a", 0, 0)
        back_pair("b", 0, 0)
        back_a(2, 1)
        back_last("a", 0, 1)
        back_fin("a", 1, 1)
        own_a(1)
        back_fin("a", 1, 0)
        back_a(1, 1)
        back_last("b", 0, 0)
        own_a(0)
        back_a(1, 0)
        back_last("b", 0, 1)
        back_fin("b", 0, 0)
        back_fin("a", 0, 0)
        out_b_own(1, 0)
        back_fin("a", 0, 1)
        back_fin("b", 0, 1)

    arrived = came[1]

    @pl.when(is_mid)
    def _():
        to_core(0, 1)
        back_fin("a", 3, 1)
        back_b(2, 2)
        back_last("a", 1, 1)
        back_a(3, 1)
        back_b(1, 1)
        core_add(0, 0)
        back_last("a", 2, 0)
        core_add(0, 1)
        back_b(2, 1)
        back_last("a", 2, 1)
        back_fin("a", 1, 0)
        back_fin("a", 2, 0)
        own_b(2)
        back_pair("a", 0, 1)
        back_fin("a", 3, 0)
        back_fin("a", 1, 1)
        back_a(3, 0)
        own_b(3)
        back_pair("a", 0, 0)
        back_b(2, 0)
        own_b(1)
        back_pair("b", 0, 1)
        back_a(1, 1)
        back_a(1, 0)
        back_fin("a", 2, 1)
        back_pair("b", 0, 0)
        back_a(2, 0)
        back_last("a", 0, 0)
        own_b(0)
        back_last("b", 0, 1)
        back_last("a", 0, 1)
        back_a(2, 1)
        back_fin("b", 0, 1)
        back_fin("a", 0, 0)
        back_last("b", 0, 0)
        own_a(1)
        back_fin("b", 0, 0)
        back_fin("a", 0, 1)
        own_a(0)

    result = pltpu.make_async_copy(parts.at[z, y, x, own], out_ref, load_sem.at[4])
    result.start()
    for condition, copy in finals:
        if condition is None:
            copy().wait_send()
        else:

            @pl.when(condition)
            def _(copy=copy):
                copy().wait_send()
    result.wait()


def dense_shards(
    tokens, expert_ids, combine, hot_flags, gate_up_weight, gate_up_scale, down_weight, down_scale
):
    planes = lax.axis_size("grp")
    lane_count = lax.axis_size("ex")
    expert_count = planes // 2 * lane_count
    rows, width = tokens.shape
    units = down_weight.shape[2]
    extra = -(-3 * expert_count // 128) * 128
    starts, sizes = column_split(width)
    a_size, b_size = sizes[0] + sizes[1], sizes[2] + sizes[3]
    bf16 = jnp.bfloat16
    dma = pltpu.SemaphoreType.DMA
    vmem = pl.BlockSpec(memory_space=pltpu.VMEM)
    return pl.pallas_call(
        functools.partial(fused_kernel, planes, expert_count),
        out_shape=jax.ShapeDtypeStruct((rows, width), bf16),
        in_specs=[
            pl.BlockSpec(memory_space=pltpu.SMEM),
            pl.BlockSpec(memory_space=pl.ANY),
            vmem,
            vmem,
            pl.BlockSpec(memory_space=pl.ANY),
            vmem,
            pl.BlockSpec(memory_space=pl.ANY),
            vmem,
        ],
        out_specs=pl.BlockSpec(memory_space=pl.ANY),
        scratch_shapes=[
            pltpu.VMEM((planes, 2, 2, 2 * rows, width + extra), bf16),
            pltpu.VMEM((planes, 2, 2, 2 * rows, width), bf16),
            pltpu.VMEM((planes, 2, 2, rows, width), bf16),
            pltpu.VMEM((planes, 2, 2, rows, max(sizes[:2])), bf16),
            pltpu.VMEM((planes, 2, rows, max(sizes[:2])), bf16),
            pltpu.VMEM((planes + 1, rows, a_size), bf16),
            pltpu.VMEM((planes + 1, 4, rows, b_size), bf16),
            pltpu.VMEM((2, 2, rows, max(sizes[2:])), bf16),
            pltpu.VMEM((2, rows, max(sizes[2:])), bf16),
            pltpu.VMEM((2, width, units), bf16),
            pltpu.VMEM((units, width), bf16),
            pltpu.VMEM((4 * rows, units), bf16),
            dma((5,)),
            dma((2, planes + 1, 2)),
            dma((2, planes + 1, 4)),
            dma((2, planes, 2, 3)),
            dma((2, 2, 3)),
            dma((2, planes, 2)),
            dma((2, planes, 2)),
            dma((2, planes, 2)),
            dma((2, planes, 2)),
            dma((2, planes + 1, 2)),
            dma((2, planes + 1, 4)),
            dma((2, 2)),
            dma((2, 2)),
        ],
        compiler_params=pltpu.CompilerParams(
            collective_id=0, has_side_effects=True, vmem_limit_bytes=67043328
        ),
    )(
        hot_flags,
        tokens,
        expert_ids.T,
        combine.T,
        gate_up_weight[0, 0],
        jnp.transpose(gate_up_scale[0, 0], (1, 0, 2)),
        down_weight[0, 0],
        down_scale[0, 0],
    )


def shards(tokens, expert_ids, *rest):
    group_count = lax.axis_size("grp")
    lane_count = lax.axis_size("ex")
    token_count = tokens.shape[0]
    expert_count = group_count // 2 * lane_count
    route_count = token_count * expert_ids.shape[1]
    capacity = max(2, (5 * route_count + 4 * expert_count - 1) // (4 * expert_count))
    chip_rows = group_count * lane_count // 2 * token_count
    if group_count == 2 * 2 and lane_count == 2 * 2 * 2 and 2 * expert_count * capacity >= chip_rows:
        return dense_shards(tokens, expert_ids, *rest)
    return routed_shards(tokens, expert_ids, *rest)


def solution(mesh):
    return jax.shard_map(
        shards,
        mesh=mesh,
        in_specs=(
            P(("grp", "ex"), None),
            P(("grp", "ex"), None),
            P(("grp", "ex"), None),
            P(),
            P("grp", "ex", None, None, None),
            P("grp", "ex", None, None, None),
            P("grp", "ex", None, None),
            P("grp", "ex", None, None),
        ),
        out_specs=P(("grp", "ex"), None),
        check_vma=False,
    )
```

```python
import functools

import jax
import jax.numpy as jnp
from jax import lax
from jax.experimental import pallas as pl
from jax.experimental.pallas import tpu as pltpu
from jax.sharding import PartitionSpec as P


def dequantize(weights, scales, is_hot):
    group_count = scales.shape[0]
    shaped = weights.reshape(group_count, weights.shape[0] // group_count, weights.shape[1])
    scaled = (shaped * scales[:, None, :]).reshape(weights.shape).astype(jnp.bfloat16)
    return jnp.where(is_hot, weights, scaled)


def routed_shards(
    tokens, expert_ids, combine, hot_flags, gate_up_weight, gate_up_scale, down_weight, down_scale
):
    group_count = lax.axis_size("grp")
    lane_count = lax.axis_size("ex")
    pair_count = group_count // 2
    token_count = tokens.shape[0]
    model_width = tokens.shape[1]
    top_count = expert_ids.shape[1]
    expert_count = pair_count * lane_count
    route_count = token_count * top_count
    capacity = max(2, (5 * route_count + 4 * expert_count - 1) // (4 * expert_count))
    slot_count = expert_count * capacity
    flat_expert = expert_ids.reshape(route_count)
    route_order = jnp.arange(route_count, dtype=jnp.int32)
    earlier = (flat_expert[None, :] == flat_expert[:, None]) & (
        route_order[None, :] < route_order[:, None]
    )
    route_rank = jnp.sum(earlier, axis=1, dtype=jnp.int32)
    slot_of = flat_expert * capacity + route_rank
    slot_match = slot_of[None, :] == jnp.arange(slot_count, dtype=jnp.int32)[:, None]
    filled = jnp.any(slot_match, axis=1)
    source = jnp.sum(jnp.where(slot_match, route_order[None, :] // top_count, 0), axis=1)
    slot_rows = jnp.where(filled[:, None], tokens[source], jnp.zeros((), tokens.dtype))
    outgoing = slot_rows.reshape(pair_count, lane_count, capacity, model_width)
    own_expert = lax.axis_index("grp") // 2 * lane_count + lax.axis_index("ex")
    is_hot = hot_flags[own_expert] == 1
    gate_matrix = dequantize(gate_up_weight[0, 0, 0], gate_up_scale[0, 0, 0], is_hot)
    up_matrix = dequantize(gate_up_weight[0, 0, 1], gate_up_scale[0, 0, 1], is_hot)
    down_matrix = dequantize(down_weight[0, 0], down_scale[0, 0], is_hot)
    pair_index = flat_expert // lane_count
    lane_index = flat_expert % lane_count
    within = lax.all_to_all(outgoing, "ex", split_axis=1, concat_axis=1, tiled=True)
    doubled = jnp.repeat(within, 2, axis=0)
    arrived_block = lax.all_to_all(doubled, "grp", split_axis=0, concat_axis=0, tiled=True)
    flat_rows = arrived_block.reshape(-1, model_width)
    gate_proj = jnp.dot(flat_rows, gate_matrix, preferred_element_type=jnp.float32)
    up_proj = jnp.dot(flat_rows, up_matrix, preferred_element_type=jnp.float32)
    hidden = (jax.nn.silu(gate_proj) * up_proj).astype(jnp.bfloat16)
    partial_value = jnp.dot(hidden, down_matrix, preferred_element_type=jnp.float32).astype(
        jnp.bfloat16
    )
    across = lax.all_to_all(
        partial_value.reshape(arrived_block.shape), "grp", split_axis=0, concat_axis=0, tiled=True
    )
    returned = lax.all_to_all(across, "ex", split_axis=1, concat_axis=1, tiled=True)
    flat_back = returned.reshape(-1, model_width)
    first_index = (2 * pair_index * lane_count + lane_index) * capacity + route_rank
    second_index = first_index + lane_count * capacity
    both_halves = flat_back[first_index].astype(jnp.float32) + flat_back[second_index].astype(
        jnp.float32
    )
    expert_rows = lax.optimization_barrier(both_halves.astype(jnp.bfloat16)).astype(jnp.float32)
    weighted = expert_rows * combine.reshape(route_count)[:, None]
    return jnp.sum(weighted.reshape(token_count, top_count, model_width), axis=1).astype(
        jnp.bfloat16
    )


def column_split(width):
    blocks = width // 128
    first = max(1, blocks * 10 // 28)
    second = max(1, (blocks - 2 * first) // 2)
    last = blocks - 2 * first - second
    starts, sizes = [], []
    at = 0
    for count in (first, first, second, last):
        starts.append(at * 128)
        sizes.append(count * 128)
        at += count
    return starts, sizes


def fused_kernel(
    planes,
    experts,
    hot_any,
    own_ref,
    ids_any,
    combine_any,
    gate_up_ref,
    gate_up_scale_any,
    down_ref,
    down_scale_any,
    out_ref,
    hot_ref,
    ids_ref,
    combine_ref,
    gate_up_scale_ref,
    down_scale_ref,
    rows_in,
    parts,
    core_in,
    pair_in,
    last_in,
    chain_a,
    chain_b,
    pair_b,
    last_b,
    gate_up,
    down,
    hidden,
    load_sem,
    chain_a_sems,
    chain_b_sems,
    spread_sems,
    spread_b_sems,
    twin_sems,
    core_sems,
    pair_sems,
    last_sems,
    back_a_sems,
    back_b_sems,
    pair_b_sems,
    last_b_sems,
):
    f32, bf16 = jnp.float32, jnp.bfloat16
    rows, width = out_ref.shape
    units = hidden.shape[1]
    extra = rows_in.shape[-1] - width
    starts, sizes = column_split(width)
    a_size = sizes[0] + sizes[1]
    b_size = sizes[2] + sizes[3]
    b_cols = pl.ds(a_size, b_size)
    b_wide = pl.ds(a_size, b_size + extra)
    cols = [pl.ds(starts[i], sizes[i]) for i in range(4)]
    wide = cols[:3] + [pl.ds(starts[3], sizes[3] + extra)]

    z = lax.axis_index("grp")
    lane = lax.axis_index("ex")
    core = lane % 2
    x = (lane // 2) % 2
    y = lane // 4
    expert = z // 2 * lax.axis_size("ex") + lane
    across_x = {"ex": lane + 2 - 4 * x}
    across_y = {"ex": lane + 4 - 8 * y}
    twin = {"ex": lane + 1 - 2 * core}
    own = pl.ds(pl.multiple_of(core * rows, rows), rows)
    others = pl.ds(pl.multiple_of((1 - core) * rows, rows), rows)
    has_up = z < planes - 1
    has_down = z > 0
    above = {"grp": jnp.minimum(z + 1, planes - 1)}
    below = {"grp": jnp.maximum(z - 1, 0)}
    room = jnp.minimum(z, planes - 1 - z)
    sign = jnp.where(z < planes - 1 - z, -1, 1)
    is_end = room == 0
    is_mid = room != 0

    def plane_of(k):
        if k == 0:
            return z
        near = z + (sign if k % 2 else -sign) * ((k + 1) // 2)
        return jnp.where(k <= 2 * room, near, z - sign * (k - room))

    groups = [plane_of(k) for k in range(planes)]
    other_x, other_y = 1 - x, 1 - y
    halves = [y, other_y]

    def mk(source, target, send_sem, recv_sem, device):
        return pltpu.make_async_remote_copy(
            src_ref=source,
            dst_ref=target,
            send_sem=send_sem,
            recv_sem=recv_sem,
            device_id=device,
            device_id_type=pl.DeviceIdType.MESH,
        )

    finals = []
    copies = {}

    def send(key, source, target, sems, index, device):
        def copy():
            return mk(source(), target(), sems.at[(0,) + index], sems.at[(1,) + index], device)

        copy().start()
        if key not in copies:
            copies[key] = copy
            finals.append((None, copy))

    def send_if(key, condition, copy):
        @pl.when(condition)
        def _():
            copy().start()

        if key not in copies:
            copies[key] = copy
            finals.append((condition, copy))

    def arrive(key):
        if key not in arrived:
            arrived.add(key)
            copies[key]().wait_recv()

    def needed(name, k, q):
        if q == 0:
            return [(name, k, t, t) for t in range(2)]
        return [(name, k, t, j) for t in range(2) for j in (1 - t, 2)]

    barrier = pltpu.get_barrier_semaphore()
    for neighbour in (across_x, across_y, twin):
        pl.semaphore_signal(
            barrier, inc=1, device_id=neighbour, device_id_type=pl.DeviceIdType.MESH
        )
    for condition, neighbour in ((has_up, above), (has_down, below)):

        @pl.when(condition)
        def _(neighbour=neighbour):
            pl.semaphore_signal(
                barrier, inc=1, device_id=neighbour, device_id_type=pl.DeviceIdType.MESH
            )

    own_copy = pltpu.make_async_copy(
        own_ref, rows_in.at[z, y, x, own, pl.ds(0, width)], load_sem.at[0]
    )
    own_copy.start()
    small = [
        pltpu.make_async_copy(source, target, load_sem.at[5 + i])
        for i, (source, target) in enumerate(
            (
                (ids_any, ids_ref),
                (combine_any, combine_ref),
                (hot_any, hot_ref),
                (gate_up_scale_any, gate_up_scale_ref),
                (down_scale_any, down_scale_ref),
            )
        )
    ]
    for copy in small:
        copy.start()
    for copy in small[:2]:
        copy.wait()
    loads = [
        pltpu.make_async_copy(gate_up_ref.at[0], gate_up.at[0], load_sem.at[1]),
        pltpu.make_async_copy(gate_up_ref.at[1], gate_up.at[1], load_sem.at[2]),
        pltpu.make_async_copy(down_ref, down, load_sem.at[3]),
    ]
    named = lax.broadcasted_iota(jnp.int32, (extra, rows), 0)
    which = named % experts
    rest = jnp.zeros((extra, rows), f32)
    for k in range(ids_ref.shape[0]):
        rest = rest + jnp.where(ids_ref[k : k + 1, :] == which, combine_ref[k : k + 1, :], 0.0)
    piece = jnp.zeros((extra, rows), f32)
    for k in range(3):
        rounded = rest.astype(bf16).astype(f32)
        piece = jnp.where((named >= k * experts) & (named < (k + 1) * experts), rounded, piece)
        rest = rest - rounded
    piece = jnp.transpose(piece)
    rows_in[z, y, x, own, pl.ds(width, extra)] = piece.astype(bf16)
    pl.semaphore_wait(barrier, 3 + has_up.astype(jnp.int32) + has_down.astype(jnp.int32))
    own_copy.wait()
    for load in loads:
        load.start()
    for copy in small[2:]:
        copy.wait()
    flag = lax.broadcasted_iota(jnp.int32, hot_ref.shape, 1) == expert
    is_hot = jnp.sum(jnp.where(flag, hot_ref[...], 0), axis=1, keepdims=True) == 1

    def out_a_own(t):
        for i, (condition, device) in enumerate(((has_up, above), (has_down, below))):

            def copy(i=i, device=device):
                block = rows_in.at[z, y, x, own, cols[t]]
                return mk(
                    block,
                    block,
                    chain_a_sems.at[0, i * planes, t],
                    chain_a_sems.at[1, z, t],
                    device,
                )

            send_if(("za", 0, t, i), condition, copy)

    def onward(k):
        g = groups[k]
        target = jnp.where(g < z, z + 1, z - 1)
        valid = (target >= 0) & (target < planes)
        return g, valid, {"grp": jnp.clip(target, 0, planes - 1)}

    onwards = [onward(k) for k in range(planes)]

    def out_a_hop(k, t):
        g, valid, device = onwards[k]

        def copy():
            block = rows_in.at[g, y, x, own, cols[t]]
            return mk(block, block, chain_a_sems.at[0, k, t], chain_a_sems.at[1, g, t], device)

        copy().wait_recv()
        send_if(("za", k, t), valid, copy)

    quarters = [(y, x), (y, other_x), (other_y, x), (other_y, other_x)]
    needed_b = [
        [],
        [("b", 0, 0, 0), ("b", 0, 1, 1)],
        [("b", 0, 1, 0), ("b", 0, 0, 1)],
        [("b", 0, 0, 2), ("b", 0, 1, 2)],
    ]

    def beside(side):
        target = z - sign if side else z + sign
        valid = (target >= 0) & (target < planes)
        return valid, {"grp": jnp.clip(target, 0, planes - 1)}

    besides = [beside(side) for side in range(2)]

    def out_b_own(c, side):
        for key in needed_b[c]:
            arrive(key)
        valid, device = besides[side]

        def copy():
            block = rows_in.at[z, quarters[c][0], quarters[c][1], own, b_wide]
            return mk(
                block,
                block,
                chain_b_sems.at[0, side * planes, c],
                chain_b_sems.at[1, z, c],
                device,
            )

        send_if(("zb", 0, c, side), valid, copy)

    def out_b_hop(k, c):
        g, valid, device = onwards[k]

        def copy():
            block = rows_in.at[g, quarters[c][0], quarters[c][1], own, b_wide]
            return mk(block, block, chain_b_sems.at[0, k, c], chain_b_sems.at[1, g, c], device)

        copy().wait_recv()
        send_if(("zb", k, c), valid, copy)

    def spread(name, k, t, j):
        sems = spread_sems if name == "a" else spread_b_sems
        base = 0 if name == "a" else 2
        index = (k, t, j) if name == "a" else (t, j)
        if j == 2:
            arrive((name, k, t, 0))
            yy, xx = (y, other_x) if t == 0 else (other_y, x)
        else:
            yy, xx = y, x

        def block():
            return rows_in.at[groups[k], yy, xx, own, wide[base + t]]

        over_x = (t + j) % 2 == 0 if j < 2 else t == 1
        send((name, k, t, j), block, block, sems, index, across_x if over_x else across_y)

    def to_twin(k, q):
        for name in ("a", "b") if k == 0 else ("a",):
            for key in needed(name, k, q):
                arrive(key)

        def block():
            return rows_in.at[groups[k], halves[q], :, own]

        send(("twin", k, q), block, block, twin_sems, (k, q), twin)

    def pick(pair):
        return jnp.where(is_end, pair[0], pair[1])

    def gate(g, h):
        tile = min(units, 256)

        def columns_of(n, carry):
            at = pl.ds(pl.multiple_of(n * tile, tile), tile)
            block = rows_in[g, h, :, :, :width].reshape(hidden.shape[0], width)
            gated = jnp.dot(block, gate_up[0, :, at], preferred_element_type=f32)
            up = jnp.dot(block, gate_up[1, :, at], preferred_element_type=f32)
            hidden[:, at] = (gated / (1.0 + jnp.exp(-gated)) * up).astype(bf16)
            return carry

        lax.fori_loop(0, units // tile, columns_of, 0)

    def project(g, h):
        tile = 512 if width % 512 == 0 else 128
        more = rows_in[g, h, :, :, width:].reshape(hidden.shape[0], -1).astype(f32)
        column = lax.broadcasted_iota(jnp.int32, more.shape, 1)
        chosen = (
            (column == expert) | (column == expert + experts) | (column == expert + 2 * experts)
        )
        weight = jnp.sum(jnp.where(chosen, more, 0.0), axis=1, keepdims=True)

        def columns_of(n, carry):
            at = pl.ds(pl.multiple_of(n * tile, tile), tile)
            value = jnp.dot(hidden[...], down[:, at], preferred_element_type=f32)
            value = jnp.where(weight != 0.0, value * weight, 0.0).astype(bf16)
            parts[g, h, :, :, at] = value.reshape(2, 2 * rows, tile)
            return carry

        lax.fori_loop(0, width // tile, columns_of, 0)

    step = 16

    def accumulate(items):
        def one(i, carry):
            at = pl.multiple_of(i * step, step)
            for (g, yy, xx), start, size, buffer, index, offset in items:
                target = (
                    g, yy, xx,
                    pl.ds(pl.multiple_of(core * rows + at, step), step),
                    pl.ds(start, size),
                )
                source = index + (pl.ds(at, step), pl.ds(offset, size))
                total = parts[target].astype(f32) + buffer[source].astype(f32)
                parts[target] = total.astype(bf16)
            return carry

        lax.fori_loop(0, rows // step, one, 0)

    def to_core(k, q):
        send(
            ("core", k, q),
            lambda: parts.at[groups[k], halves[q], :, others],
            lambda: core_in.at[k, q],
            core_sems,
            (k, q),
            twin,
        )

    def core_add(k, q):
        arrive(("core", k, q))
        accumulate(
            [((groups[k], halves[q], i), 0, width, core_in, (k, q, i), 0) for i in range(2)]
        )

    def back_pair(name, k, t):
        g = groups[k]
        c = (0 if name == "a" else 2) + t
        sems = pair_sems if name == "a" else pair_b_sems
        index = (k, t) if name == "a" else (t,)

        def source():
            if t == 0:
                return parts.at[g, other_y, :, own, cols[c]]
            return parts.at[g, :, other_x, own, cols[c]]

        def target():
            ref = pair_in if name == "a" else pair_b
            return ref.at[index + (slice(None), slice(None), pl.ds(0, sizes[c]))]

        device = across_y if t == 0 else across_x
        send(("pair", name, k, t), source, target, sems, index, device)

    def back_last(name, k, t):
        g = groups[k]
        c = (0 if name == "a" else 2) + t
        sems = last_sems if name == "a" else last_b_sems
        index = (k, t) if name == "a" else (t,)
        arrive(("pair", name, k, t))
        buffer = pair_in if name == "a" else pair_b
        accumulate(
            [
                ((g, y, i) if t == 0 else (g, i, x), starts[c], sizes[c], buffer, index + (i,), 0)
                for i in range(2)
            ]
        )

        def source():
            if t == 0:
                return parts.at[g, y, other_x, own, cols[c]]
            return parts.at[g, other_y, x, own, cols[c]]

        def target():
            ref = last_in if name == "a" else last_b
            return ref.at[index + (slice(None), pl.ds(0, sizes[c]))]

        device = across_x if t == 0 else across_y
        send(("last", name, k, t), source, target, sems, index, device)

    def back_fin(name, k, t):
        c = (0 if name == "a" else 2) + t
        source = last_in if name == "a" else last_b
        index = (k, t) if name == "a" else (t,)
        arrive(("last", name, k, t))
        accumulate([((groups[k], y, x), starts[c], sizes[c], source, index, 0)])

    def inward(k):
        g = groups[k]
        falling = g < z
        source = jnp.where(falling, z + 1, z - 1)
        target = jnp.where(falling, z - 1, z + 1)
        valid = (source >= 0) & (source < planes)
        slot = jnp.where((target == g) & falling, planes, g)
        return g, valid, {"grp": jnp.clip(target, 0, planes - 1)}, slot

    inwards = [inward(k) for k in range(planes)]

    def back_a(k, t):
        g, valid, device, slot = inwards[k]

        @pl.when(valid)
        def _():
            block = chain_a.at[g, :, cols[t]]
            sem = back_a_sems.at
            mk(block, block, sem[0, k, t], sem[1, g, t], device).wait_recv()
            accumulate([((g, y, x), starts[t], sizes[t], chain_a, (g,), starts[t])])

        def copy():
            return mk(
                parts.at[g, y, x, own, cols[t]],
                chain_a.at[slot, :, cols[t]],
                back_a_sems.at[0, k, t],
                back_a_sems.at[1, slot, t],
                device,
            )

        copy().start()
        if ("ra", k, t) not in copies:
            copies["ra", k, t] = copy
            finals.append((None, copy))

    def back_b(k, c):
        g, valid, device, slot = inwards[k]
        yy, xx = quarters[c]

        @pl.when(valid)
        def _():
            block = chain_b.at[g, c]
            sem = back_b_sems.at
            mk(block, block, sem[0, k, c], sem[1, g, c], device).wait_recv()
            accumulate([((g, yy, xx), a_size, b_size, chain_b, (g, c), 0)])

        def copy():
            return mk(
                parts.at[g, yy, xx, own, b_cols],
                chain_b.at[slot, c],
                back_b_sems.at[0, k, c],
                back_b_sems.at[1, slot, c],
                device,
            )

        copy().start()
        if ("rb", k, c) not in copies:
            copies["rb", k, c] = copy
            finals.append((None, copy))

    def own_sides():
        return ((has_down, z, below), (has_up, planes, above))

    def own_b(c):
        for condition, slot, device in own_sides():

            @pl.when(condition)
            def _(slot=slot, device=device):
                block = chain_b.at[slot, c]
                sem = back_b_sems.at
                mk(block, block, sem[0, 0, c], sem[1, slot, c], device).wait_recv()
                accumulate([((z, *quarters[c]), a_size, b_size, chain_b, (slot, c), 0)])

    def own_a(t):
        for condition, slot, device in own_sides():

            @pl.when(condition)
            def _(slot=slot, device=device):
                block = chain_a.at[slot, :, pl.ds(starts[t], sizes[t])]
                sem = back_a_sems.at
                mk(block, block, sem[0, 0, t], sem[1, slot, t], device).wait_recv()
                accumulate([((z, y, x), starts[t], sizes[t], chain_a, (slot,), starts[t])])

    def scale_rows(ref, scale_of, count):
        size = ref.shape[0] // count

        def one(g, carry):
            at = pl.ds(pl.multiple_of(g * size, size), size)
            scale = jnp.where(is_hot, 1.0, scale_of(g))
            ref[at] = (ref[at].astype(f32) * scale).astype(bf16)
            return carry

        lax.fori_loop(0, count, one, 0)

    def scale_gate_up(j):
        loads[1 if j else 0].wait()
        scale_rows(
            gate_up.at[j],
            lambda g: gate_up_scale_ref[g, pl.ds(j, 1), :],
            gate_up_scale_ref.shape[0],
        )

    def scale_down():
        loads[2].wait()
        scale_rows(down, lambda g: down_scale_ref[pl.ds(g, 1), :], down_scale_ref.shape[0])

    came = [set(), set()]

    arrived = came[0]

    @pl.when(is_end)
    def _():
        spread("a", 0, 1, 0)
        spread("b", 0, 1, 0)
        out_a_own(1)
        spread("a", 0, 0, 0)
        spread("a", 0, 0, 1)
        spread("a", 0, 1, 1)
        out_a_own(0)
        out_a_hop(1, 0)
        spread("b", 0, 0, 1)
        spread("a", 0, 0, 2)
        spread("b", 0, 1, 1)
        out_b_own(0, 1)
        spread("b", 0, 0, 0)
        scale_down()
        spread("b", 0, 1, 2)
        spread("b", 0, 0, 2)
        to_twin(0, 0)
        out_a_hop(1, 1)
        out_a_hop(2, 0)
        spread("a", 2, 0, 0)
        out_b_own(1, 1)
        spread("a", 2, 0, 1)
        scale_gate_up(1)
        spread("a", 0, 1, 2)
        scale_gate_up(0)
        out_a_hop(2, 1)
        out_b_own(2, 1)
        arrive(("twin", 0, 0))

    arrived = came[1]

    @pl.when(is_mid)
    def _():
        out_a_own(0)
        spread("b", 0, 0, 0)
        spread("b", 0, 1, 0)
        out_a_own(1)
        spread("b", 0, 0, 2)
        spread("a", 0, 0, 0)
        scale_gate_up(0)
        scale_down()
        out_a_hop(1, 1)
        spread("a", 1, 1, 0)
        spread("a", 1, 1, 1)
        out_a_hop(2, 0)
        spread("a", 2, 0, 1)
        spread("b", 0, 0, 1)
        out_a_hop(2, 1)
        spread("b", 0, 1, 2)
        out_a_hop(1, 0)
        spread("a", 1, 0, 0)
        scale_gate_up(1)
        out_a_hop(3, 1)
        out_b_hop(1, 0)
        spread("a", 3, 1, 0)
        spread("a", 3, 1, 1)
        spread("a", 2, 1, 0)
        out_b_hop(1, 1)
        out_a_hop(3, 0)
        spread("a", 3, 0, 1)
        spread("a", 1, 0, 1)
        spread("a", 3, 0, 0)
        out_b_hop(1, 2)
        out_b_hop(3, 0)
        spread("b", 0, 1, 1)
        to_twin(1, 0)
        out_b_hop(3, 1)
        out_b_hop(1, 3)
        to_twin(3, 0)
        spread("a", 3, 0, 2)
        spread("a", 3, 1, 2)
        spread("a", 1, 1, 2)
        out_b_own(3, 1)
        out_b_hop(3, 2)
        arrive(("twin", 1, 0))

    at_group = pick((groups[0], groups[1]))
    at_half = pick((halves[0], halves[0]))
    gate(at_group, at_half)

    arrived = came[0]

    @pl.when(is_end)
    def _():
        out_a_hop(3, 1)
        out_b_own(3, 1)
        spread("a", 3, 1, 0)
        spread("a", 3, 1, 1)

    arrived = came[1]

    @pl.when(is_mid)
    def _():
        out_b_own(2, 1)
    project(at_group, at_half)

    arrived = came[0]

    @pl.when(is_end)
    def _():
        to_core(0, 0)
        spread("a", 2, 1, 0)
        out_a_hop(3, 0)
        spread("a", 3, 0, 0)
        to_twin(0, 1)
        spread("a", 3, 1, 2)
        spread("a", 3, 0, 1)
        arrive(("twin", 0, 1))

    arrived = came[1]

    @pl.when(is_mid)
    def _():
        to_core(1, 0)
        out_b_own(1, 1)
        out_b_hop(3, 3)
        spread("a", 2, 1, 1)
        spread("a", 0, 1, 0)
        spread("a", 2, 0, 0)
        out_b_own(0, 1)
        spread("a", 0, 1, 1)
        arrive(("twin", 3, 0))

    at_group = pick((groups[0], groups[3]))
    at_half = pick((halves[1], halves[0]))
    gate(at_group, at_half)

    arrived = came[0]

    @pl.when(is_end)
    def _():
        out_b_hop(3, 1)
        spread("a", 3, 0, 2)
        out_b_hop(3, 0)
        spread("a", 2, 0, 2)
        spread("a", 1, 1, 0)
        out_b_own(1, 0)
        to_twin(3, 0)
        spread("a", 2, 1, 2)
        spread("a", 1, 0, 0)

    arrived = came[1]

    @pl.when(is_mid)
    def _():
        spread("a", 1, 0, 2)
        to_twin(3, 1)
        out_b_hop(2, 3)
        out_b_hop(2, 2)
    project(at_group, at_half)

    arrived = came[0]

    @pl.when(is_end)
    def _():
        to_core(0, 1)
        spread("a", 2, 1, 1)
        out_b_hop(3, 2)
        arrive(("twin", 3, 0))

    arrived = came[1]

    @pl.when(is_mid)
    def _():
        to_core(3, 0)
        out_b_hop(2, 1)
        spread("a", 0, 0, 2)
        arrive(("twin", 3, 1))

    at_group = pick((groups[3], groups[3]))
    at_half = pick((halves[0], halves[1]))
    gate(at_group, at_half)

    arrived = came[0]

    @pl.when(is_end)
    def _():
        spread("a", 1, 1, 1)
        spread("a", 1, 0, 1)
        out_b_hop(3, 3)
        to_twin(3, 1)
        core_add(0, 0)

    arrived = came[1]

    @pl.when(is_mid)
    def _():
        to_twin(1, 1)
        core_add(3, 0)
        out_b_hop(2, 0)
        spread("a", 2, 0, 2)
        spread("a", 2, 1, 2)
        spread("a", 0, 1, 2)
        out_b_own(2, 0)
        out_b_own(3, 0)
    project(at_group, at_half)

    arrived = came[0]

    @pl.when(is_end)
    def _():
        to_core(3, 0)
        out_b_hop(2, 3)
        arrive(("twin", 3, 1))

    arrived = came[1]

    @pl.when(is_mid)
    def _():
        to_core(3, 1)
        spread("a", 0, 0, 1)
        arrive(("twin", 1, 1))

    at_group = pick((groups[3], groups[1]))
    at_half = pick((halves[1], halves[1]))
    gate(at_group, at_half)

    arrived = came[0]

    @pl.when(is_end)
    def _():
        out_b_hop(2, 2)
        out_b_own(2, 0)
        to_twin(2, 1)
        core_add(3, 0)
        back_b(3, 0)
        spread("a", 1, 0, 2)
        spread("a", 1, 1, 2)
        back_b(3, 1)

    arrived = came[1]

    @pl.when(is_mid)
    def _():
        core_add(3, 1)
        to_twin(2, 1)
    project(at_group, at_half)

    arrived = came[0]

    @pl.when(is_end)
    def _():
        to_core(3, 1)
        out_b_hop(2, 1)
        arrive(("twin", 2, 1))

    arrived = came[1]

    @pl.when(is_mid)
    def _():
        to_core(1, 1)
        out_b_own(1, 0)
        back_b(3, 1)
        core_add(1, 0)
        back_pair("a", 3, 0)
        back_pair("a", 3, 1)
        arrive(("twin", 2, 1))

    at_group = pick((groups[2], groups[2]))
    at_half = pick((halves[1], halves[1]))
    gate(at_group, at_half)

    arrived = came[0]

    @pl.when(is_end)
    def _():
        out_b_hop(2, 0)
        to_twin(2, 0)
        core_add(3, 1)
        back_pair("a", 3, 0)
        back_b(3, 2)
        back_pair("a", 3, 1)

    arrived = came[1]

    @pl.when(is_mid)
    def _():
        to_twin(2, 0)
        core_add(1, 1)
        out_b_own(0, 0)
        back_b(3, 0)
        back_pair("a", 1, 0)
    project(at_group, at_half)

    arrived = came[0]

    @pl.when(is_end)
    def _():
        to_core(2, 1)
        back_b(3, 3)
        arrive(("twin", 2, 0))

    arrived = came[1]

    @pl.when(is_mid)
    def _():
        to_core(2, 1)
        back_b(3, 2)
        back_pair("a", 1, 1)
        arrive(("twin", 2, 0))

    at_group = pick((groups[2], groups[2]))
    at_half = pick((halves[0], halves[0]))
    gate(at_group, at_half)

    arrived = came[0]

    @pl.when(is_end)
    def _():
        core_add(2, 1)
        back_b(2, 2)
        back_pair("a", 2, 0)

    arrived = came[1]

    @pl.when(is_mid)
    def _():
        to_twin(0, 1)
        back_last("a", 3, 0)
        core_add(2, 1)
        back_pair("a", 2, 0)
        to_twin(0, 0)
        back_b(1, 0)
        back_b(3, 3)
    project(at_group, at_half)

    arrived = came[0]

    @pl.when(is_end)
    def _():
        to_core(2, 0)
        out_b_hop(1, 3)
        back_last("a", 3, 0)
        back_b(2, 3)
        core_add(2, 0)
        out_b_own(0, 0)
        back_b(2, 0)
        back_pair("a", 2, 1)
        back_last("a", 3, 1)
        out_b_hop(1, 0)
        out_b_hop(1, 2)
        out_b_own(3, 0)
        to_twin(1, 1)
        core_add(0, 1)
        out_b_hop(1, 1)
        back_pair("a", 0, 0)
        back_fin("a", 3, 0)
        back_b(2, 1)
        back_pair("a", 0, 1)
        back_a(3, 0)
        to_twin(1, 0)
        arrive(("twin", 1, 1))

    arrived = came[1]

    @pl.when(is_mid)
    def _():
        to_core(2, 0)
        arrive(("twin", 0, 1))

    at_group = pick((groups[1], groups[0]))
    at_half = pick((halves[1], halves[1]))
    gate(at_group, at_half)

    arrived = came[1]

    @pl.when(is_mid)
    def _():
        back_b(1, 3)
        back_b(2, 3)
    project(at_group, at_half)

    arrived = came[0]

    @pl.when(is_end)
    def _():
        to_core(1, 1)
        back_fin("a", 3, 1)
        back_a(3, 1)
        arrive(("twin", 1, 0))

    arrived = came[1]

    @pl.when(is_mid)
    def _():
        to_core(0, 1)
        back_b(1, 2)
        core_add(2, 0)
        back_last("a", 1, 0)
        arrive(("twin", 0, 0))

    at_group = pick((groups[1], groups[0]))
    at_half = pick((halves[0], halves[0]))
    gate(at_group, at_half)

    arrived = came[0]

    @pl.when(is_end)
    def _():
        back_last("a", 2, 0)
        back_last("a", 2, 1)
        core_add(1, 1)
        back_b(1, 2)

    arrived = came[1]

    @pl.when(is_mid)
    def _():
        back_pair("a", 2, 1)
        back_last("a", 3, 1)
        back_b(2, 1)
        back_last("a", 2, 0)
        back_b(1, 1)
        back_fin("a", 3, 0)
        core_add(0, 1)
    project(at_group, at_half)

    arrived = came[0]

    @pl.when(is_end)
    def _():
        to_core(1, 0)
        own_b(2)
        back_b(1, 3)
        back_pair("a", 1, 0)
        core_add(1, 0)
        back_pair("a", 1, 1)
        own_b(1)
        back_b(1, 0)
        back_b(1, 1)
        back_fin("a", 2, 0)
        back_fin("a", 2, 1)
        own_b(0)
        own_b(3)
        back_a(2, 0)
        back_a(2, 1)
        back_pair("b", 0, 0)
        back_last("a", 1, 0)
        back_last("a", 1, 1)
        back_pair("b", 0, 1)
        back_fin("a", 1, 0)
        back_last("a", 0, 0)
        back_last("a", 0, 1)
        back_a(1, 0)
        back_fin("a", 1, 1)
        own_a(1)
        back_last("b", 0, 0)
        back_a(1, 1)
        back_last("b", 0, 1)
        own_a(0)
        back_fin("b", 0, 1)
        back_fin("a", 0, 0)
        back_fin("a", 0, 1)
        back_fin("b", 0, 0)

    arrived = came[1]

    @pl.when(is_mid)
    def _():
        to_core(0, 0)
        back_b(2, 2)
        back_b(2, 0)
        back_last("a", 1, 1)
        core_add(0, 0)
        back_fin("a", 3, 1)
        back_pair("a", 0, 1)
        back_pair("a", 0, 0)
        back_a(3, 1)
        back_fin("a", 1, 1)
        back_a(3, 0)
        back_fin("a", 1, 0)
        back_a(1, 1)
        own_b(1)
        own_b(2)
        back_last("a", 2, 1)
        own_b(3)
        own_b(0)
        back_pair("b", 0, 1)
        back_pair("b", 0, 0)
        back_last("a", 0, 0)
        back_fin("a", 2, 0)
        back_a(1, 0)
        back_a(2, 0)
        back_last("a", 0, 1)
        back_last("b", 0, 1)
        back_last("b", 0, 0)
        back_fin("a", 2, 1)
        back_a(2, 1)
        own_a(0)
        back_fin("b", 0, 0)
        back_fin("a", 0, 1)
        back_fin("b", 0, 1)
        back_fin("a", 0, 0)
        own_a(1)

    result = pltpu.make_async_copy(parts.at[z, y, x, own], out_ref, load_sem.at[4])
    result.start()
    for condition, copy in finals:
        if condition is None:
            copy().wait_send()
        else:

            @pl.when(condition)
            def _(copy=copy):
                copy().wait_send()
    result.wait()


def dense_shards(
    tokens, expert_ids, combine, hot_flags, gate_up_weight, gate_up_scale, down_weight, down_scale
):
    planes = lax.axis_size("grp")
    lane_count = lax.axis_size("ex")
    expert_count = planes // 2 * lane_count
    rows, width = tokens.shape
    units = down_weight.shape[2]
    extra = -(-3 * expert_count // 128) * 128
    starts, sizes = column_split(width)
    a_size, b_size = sizes[0] + sizes[1], sizes[2] + sizes[3]
    bf16 = jnp.bfloat16
    dma = pltpu.SemaphoreType.DMA
    return pl.pallas_call(
        functools.partial(fused_kernel, planes, expert_count),
        out_shape=jax.ShapeDtypeStruct((rows, width), bf16),
        in_specs=[pl.BlockSpec(memory_space=pl.ANY)] * 8,
        out_specs=pl.BlockSpec(memory_space=pl.ANY),
        scratch_shapes=[
            pltpu.VMEM((1, expert_count), jnp.int32),
            pltpu.VMEM(expert_ids.shape[::-1], jnp.int32),
            pltpu.VMEM(combine.shape[::-1], jnp.float32),
            pltpu.VMEM((gate_up_scale.shape[3], 2, units), jnp.float32),
            pltpu.VMEM(down_scale.shape[2:], jnp.float32),
            pltpu.VMEM((planes, 2, 2, 2 * rows, width + extra), bf16),
            pltpu.VMEM((planes, 2, 2, 2 * rows, width), bf16),
            pltpu.VMEM((planes, 2, 2, rows, width), bf16),
            pltpu.VMEM((planes, 2, 2, rows, max(sizes[:2])), bf16),
            pltpu.VMEM((planes, 2, rows, max(sizes[:2])), bf16),
            pltpu.VMEM((planes + 1, rows, a_size), bf16),
            pltpu.VMEM((planes + 1, 4, rows, b_size), bf16),
            pltpu.VMEM((2, 2, rows, max(sizes[2:])), bf16),
            pltpu.VMEM((2, rows, max(sizes[2:])), bf16),
            pltpu.VMEM((2, width, units), bf16),
            pltpu.VMEM((units, width), bf16),
            pltpu.VMEM((4 * rows, units), bf16),
            dma((10,)),
            dma((2, planes + 1, 2)),
            dma((2, planes + 1, 4)),
            dma((2, planes, 2, 3)),
            dma((2, 2, 3)),
            dma((2, planes, 2)),
            dma((2, planes, 2)),
            dma((2, planes, 2)),
            dma((2, planes, 2)),
            dma((2, planes + 1, 2)),
            dma((2, planes + 1, 4)),
            dma((2, 2)),
            dma((2, 2)),
        ],
        compiler_params=pltpu.CompilerParams(
            collective_id=0, has_side_effects=True, vmem_limit_bytes=67043328
        ),
    )(
        hot_flags.reshape(1, -1),
        tokens,
        expert_ids.T,
        combine.T,
        gate_up_weight[0, 0],
        jnp.transpose(gate_up_scale[0, 0], (1, 0, 2)),
        down_weight[0, 0],
        down_scale[0, 0],
    )


def shards(tokens, expert_ids, *rest):
    group_count = lax.axis_size("grp")
    lane_count = lax.axis_size("ex")
    token_count = tokens.shape[0]
    expert_count = group_count // 2 * lane_count
    route_count = token_count * expert_ids.shape[1]
    capacity = max(2, (5 * route_count + 4 * expert_count - 1) // (4 * expert_count))
    chip_rows = group_count * lane_count // 2 * token_count
    if group_count == 2 * 2 and lane_count == 2 * 2 * 2 and 2 * expert_count * capacity >= chip_rows:
        return dense_shards(tokens, expert_ids, *rest)
    return routed_shards(tokens, expert_ids, *rest)


def solution(mesh):
    return jax.shard_map(
        shards,
        mesh=mesh,
        in_specs=(
            P(("grp", "ex"), None),
            P(("grp", "ex"), None),
            P(("grp", "ex"), None),
            P(),
            P("grp", "ex", None, None, None),
            P("grp", "ex", None, None, None),
            P("grp", "ex", None, None),
            P("grp", "ex", None, None),
        ),
        out_specs=P(("grp", "ex"), None),
        check_vma=False,
    )
```

```python
import functools

import jax
import jax.numpy as jnp
from jax import lax
from jax.experimental import pallas as pl
from jax.experimental.pallas import tpu as pltpu
from jax.sharding import PartitionSpec as P


def dequantize(weights, scales, is_hot):
    group_count = scales.shape[0]
    shaped = weights.reshape(group_count, weights.shape[0] // group_count, weights.shape[1])
    scaled = (shaped * scales[:, None, :]).reshape(weights.shape).astype(jnp.bfloat16)
    return jnp.where(is_hot, weights, scaled)


def routed_shards(
    tokens, expert_ids, combine, hot_flags, gate_up_weight, gate_up_scale, down_weight, down_scale
):
    group_count = lax.axis_size("grp")
    lane_count = lax.axis_size("ex")
    pair_count = group_count // 2
    token_count = tokens.shape[0]
    model_width = tokens.shape[1]
    top_count = expert_ids.shape[1]
    expert_count = pair_count * lane_count
    route_count = token_count * top_count
    capacity = max(2, (5 * route_count + 4 * expert_count - 1) // (4 * expert_count))
    slot_count = expert_count * capacity
    flat_expert = expert_ids.reshape(route_count)
    route_order = jnp.arange(route_count, dtype=jnp.int32)
    earlier = (flat_expert[None, :] == flat_expert[:, None]) & (
        route_order[None, :] < route_order[:, None]
    )
    route_rank = jnp.sum(earlier, axis=1, dtype=jnp.int32)
    slot_of = flat_expert * capacity + route_rank
    slot_match = slot_of[None, :] == jnp.arange(slot_count, dtype=jnp.int32)[:, None]
    filled = jnp.any(slot_match, axis=1)
    source = jnp.sum(jnp.where(slot_match, route_order[None, :] // top_count, 0), axis=1)
    slot_rows = jnp.where(filled[:, None], tokens[source], jnp.zeros((), tokens.dtype))
    outgoing = slot_rows.reshape(pair_count, lane_count, capacity, model_width)
    own_expert = lax.axis_index("grp") // 2 * lane_count + lax.axis_index("ex")
    is_hot = hot_flags[own_expert] == 1
    gate_matrix = dequantize(gate_up_weight[0, 0, 0], gate_up_scale[0, 0, 0], is_hot)
    up_matrix = dequantize(gate_up_weight[0, 0, 1], gate_up_scale[0, 0, 1], is_hot)
    down_matrix = dequantize(down_weight[0, 0], down_scale[0, 0], is_hot)
    pair_index = flat_expert // lane_count
    lane_index = flat_expert % lane_count
    within = lax.all_to_all(outgoing, "ex", split_axis=1, concat_axis=1, tiled=True)
    doubled = jnp.repeat(within, 2, axis=0)
    arrived_block = lax.all_to_all(doubled, "grp", split_axis=0, concat_axis=0, tiled=True)
    flat_rows = arrived_block.reshape(-1, model_width)
    gate_proj = jnp.dot(flat_rows, gate_matrix, preferred_element_type=jnp.float32)
    up_proj = jnp.dot(flat_rows, up_matrix, preferred_element_type=jnp.float32)
    hidden = (jax.nn.silu(gate_proj) * up_proj).astype(jnp.bfloat16)
    partial_value = jnp.dot(hidden, down_matrix, preferred_element_type=jnp.float32).astype(
        jnp.bfloat16
    )
    across = lax.all_to_all(
        partial_value.reshape(arrived_block.shape), "grp", split_axis=0, concat_axis=0, tiled=True
    )
    returned = lax.all_to_all(across, "ex", split_axis=1, concat_axis=1, tiled=True)
    flat_back = returned.reshape(-1, model_width)
    first_index = (2 * pair_index * lane_count + lane_index) * capacity + route_rank
    second_index = first_index + lane_count * capacity
    both_halves = flat_back[first_index].astype(jnp.float32) + flat_back[second_index].astype(
        jnp.float32
    )
    expert_rows = lax.optimization_barrier(both_halves.astype(jnp.bfloat16)).astype(jnp.float32)
    weighted = expert_rows * combine.reshape(route_count)[:, None]
    return jnp.sum(weighted.reshape(token_count, top_count, model_width), axis=1).astype(
        jnp.bfloat16
    )


def column_split(width):
    blocks = width // 128
    first = max(1, blocks * 10 // 28)
    second = max(1, (blocks - 2 * first) // 2)
    last = blocks - 2 * first - second
    starts, sizes = [], []
    at = 0
    for count in (first, first, second, last):
        starts.append(at * 128)
        sizes.append(count * 128)
        at += count
    return starts, sizes


def fused_kernel(
    planes,
    experts,
    hot_any,
    own_ref,
    ids_any,
    combine_any,
    gate_up_ref,
    gate_up_scale_any,
    down_ref,
    down_scale_any,
    out_ref,
    hot_ref,
    ids_ref,
    combine_ref,
    gate_up_scale_ref,
    down_scale_ref,
    rows_in,
    parts,
    core_in,
    pair_in,
    last_in,
    chain_a,
    chain_b,
    pair_b,
    last_b,
    gate_up,
    down,
    hidden,
    load_sem,
    chain_a_sems,
    chain_b_sems,
    spread_sems,
    spread_b_sems,
    twin_sems,
    core_sems,
    pair_sems,
    last_sems,
    back_a_sems,
    back_b_sems,
    pair_b_sems,
    last_b_sems,
):
    f32, bf16 = jnp.float32, jnp.bfloat16
    rows, width = out_ref.shape
    units = hidden.shape[1]
    extra = rows_in.shape[-1] - width
    starts, sizes = column_split(width)
    a_size = sizes[0] + sizes[1]
    b_size = sizes[2] + sizes[3]
    b_cols = pl.ds(a_size, b_size)
    b_wide = pl.ds(a_size, b_size + extra)
    cols = [pl.ds(starts[i], sizes[i]) for i in range(4)]
    wide = cols[:3] + [pl.ds(starts[3], sizes[3] + extra)]

    z = lax.axis_index("grp")
    lane = lax.axis_index("ex")
    core = lane % 2
    x = (lane // 2) % 2
    y = lane // 4
    expert = z // 2 * lax.axis_size("ex") + lane
    across_x = {"ex": lane + 2 - 4 * x}
    across_y = {"ex": lane + 4 - 8 * y}
    twin = {"ex": lane + 1 - 2 * core}
    own = pl.ds(pl.multiple_of(core * rows, rows), rows)
    others = pl.ds(pl.multiple_of((1 - core) * rows, rows), rows)
    has_up = z < planes - 1
    has_down = z > 0
    above = {"grp": jnp.minimum(z + 1, planes - 1)}
    below = {"grp": jnp.maximum(z - 1, 0)}
    room = jnp.minimum(z, planes - 1 - z)
    sign = jnp.where(z < planes - 1 - z, -1, 1)
    is_end = room == 0
    is_mid = room != 0

    def plane_of(k):
        if k == 0:
            return z
        near = z + (sign if k % 2 else -sign) * ((k + 1) // 2)
        return jnp.where(k <= 2 * room, near, z - sign * (k - room))

    groups = [plane_of(k) for k in range(planes)]
    other_x, other_y = 1 - x, 1 - y
    halves = [y, other_y]

    def mk(source, target, send_sem, recv_sem, device):
        return pltpu.make_async_remote_copy(
            src_ref=source,
            dst_ref=target,
            send_sem=send_sem,
            recv_sem=recv_sem,
            device_id=device,
            device_id_type=pl.DeviceIdType.MESH,
        )

    finals = []
    copies = {}

    def send(key, source, target, sems, index, device):
        def copy():
            return mk(source(), target(), sems.at[(0,) + index], sems.at[(1,) + index], device)

        copy().start()
        if key not in copies:
            copies[key] = copy
            finals.append((None, copy))

    def send_if(key, condition, copy):
        @pl.when(condition)
        def _():
            copy().start()

        if key not in copies:
            copies[key] = copy
            finals.append((condition, copy))

    def arrive(key):
        if key not in arrived:
            arrived.add(key)
            copies[key]().wait_recv()

    def needed(name, k, q):
        if q == 0:
            return [(name, k, t, t) for t in range(2)]
        return [(name, k, t, j) for t in range(2) for j in (1 - t, 2)]

    barrier = pltpu.get_barrier_semaphore()
    for neighbour in (across_x, across_y, twin):
        pl.semaphore_signal(
            barrier, inc=1, device_id=neighbour, device_id_type=pl.DeviceIdType.MESH
        )
    for condition, neighbour in ((has_up, above), (has_down, below)):

        @pl.when(condition)
        def _(neighbour=neighbour):
            pl.semaphore_signal(
                barrier, inc=1, device_id=neighbour, device_id_type=pl.DeviceIdType.MESH
            )

    own_copy = pltpu.make_async_copy(
        own_ref, rows_in.at[z, y, x, own, pl.ds(0, width)], load_sem.at[0]
    )
    own_copy.start()
    small = [
        pltpu.make_async_copy(source, target, load_sem.at[5 + i])
        for i, (source, target) in enumerate(
            (
                (ids_any, ids_ref),
                (combine_any, combine_ref),
                (hot_any, hot_ref),
                (gate_up_scale_any, gate_up_scale_ref),
                (down_scale_any, down_scale_ref),
            )
        )
    ]
    for copy in small:
        copy.start()
    for copy in small[:2]:
        copy.wait()
    loads = [
        pltpu.make_async_copy(gate_up_ref.at[0], gate_up.at[0], load_sem.at[1]),
        pltpu.make_async_copy(gate_up_ref.at[1], gate_up.at[1], load_sem.at[2]),
        pltpu.make_async_copy(down_ref, down, load_sem.at[3]),
    ]
    named = lax.broadcasted_iota(jnp.int32, (extra, rows), 0)
    which = named % experts
    rest = jnp.zeros((extra, rows), f32)
    for k in range(ids_ref.shape[0]):
        rest = rest + jnp.where(ids_ref[k : k + 1, :] == which, combine_ref[k : k + 1, :], 0.0)
    piece = jnp.zeros((extra, rows), f32)
    for k in range(3):
        rounded = rest.astype(bf16).astype(f32)
        piece = jnp.where((named >= k * experts) & (named < (k + 1) * experts), rounded, piece)
        rest = rest - rounded
    piece = jnp.transpose(piece)
    rows_in[z, y, x, own, pl.ds(width, extra)] = piece.astype(bf16)
    pl.semaphore_wait(barrier, 3 + has_up.astype(jnp.int32) + has_down.astype(jnp.int32))
    own_copy.wait()
    for load in loads:
        load.start()
    for copy in small[2:]:
        copy.wait()
    flag = lax.broadcasted_iota(jnp.int32, hot_ref.shape, 1) == expert
    is_hot = jnp.sum(jnp.where(flag, hot_ref[...], 0), axis=1, keepdims=True) == 1

    def out_a_own(t):
        for i, (condition, device) in enumerate(((has_up, above), (has_down, below))):

            def copy(i=i, device=device):
                block = rows_in.at[z, y, x, own, cols[t]]
                return mk(
                    block,
                    block,
                    chain_a_sems.at[0, i * planes, t],
                    chain_a_sems.at[1, z, t],
                    device,
                )

            send_if(("za", 0, t, i), condition, copy)

    def onward(k):
        g = groups[k]
        target = jnp.where(g < z, z + 1, z - 1)
        valid = (target >= 0) & (target < planes)
        return g, valid, {"grp": jnp.clip(target, 0, planes - 1)}

    onwards = [onward(k) for k in range(planes)]

    def out_a_hop(k, t):
        g, valid, device = onwards[k]

        def copy():
            block = rows_in.at[g, y, x, own, cols[t]]
            return mk(block, block, chain_a_sems.at[0, k, t], chain_a_sems.at[1, g, t], device)

        copy().wait_recv()
        send_if(("za", k, t), valid, copy)

    quarters = [(y, x), (y, other_x), (other_y, x), (other_y, other_x)]
    needed_b = [
        [],
        [("b", 0, 0, 0), ("b", 0, 1, 1)],
        [("b", 0, 1, 0), ("b", 0, 0, 1)],
        [("b", 0, 0, 2), ("b", 0, 1, 2)],
    ]

    def beside(side):
        target = z - sign if side else z + sign
        valid = (target >= 0) & (target < planes)
        return valid, {"grp": jnp.clip(target, 0, planes - 1)}

    besides = [beside(side) for side in range(2)]

    def out_b_own(c, side):
        for key in needed_b[c]:
            arrive(key)
        valid, device = besides[side]

        def copy():
            block = rows_in.at[z, quarters[c][0], quarters[c][1], own, b_wide]
            return mk(
                block,
                block,
                chain_b_sems.at[0, side * planes, c],
                chain_b_sems.at[1, z, c],
                device,
            )

        send_if(("zb", 0, c, side), valid, copy)

    def out_b_hop(k, c):
        g, valid, device = onwards[k]

        def copy():
            block = rows_in.at[g, quarters[c][0], quarters[c][1], own, b_wide]
            return mk(block, block, chain_b_sems.at[0, k, c], chain_b_sems.at[1, g, c], device)

        copy().wait_recv()
        send_if(("zb", k, c), valid, copy)

    def spread(name, k, t, j):
        sems = spread_sems if name == "a" else spread_b_sems
        base = 0 if name == "a" else 2
        index = (k, t, j) if name == "a" else (t, j)
        if j == 2:
            arrive((name, k, t, 0))
            yy, xx = (y, other_x) if t == 0 else (other_y, x)
        else:
            yy, xx = y, x

        def block():
            return rows_in.at[groups[k], yy, xx, own, wide[base + t]]

        over_x = (t + j) % 2 == 0 if j < 2 else t == 1
        send((name, k, t, j), block, block, sems, index, across_x if over_x else across_y)

    def to_twin(k, q):
        for name in ("a", "b") if k == 0 else ("a",):
            for key in needed(name, k, q):
                arrive(key)

        def block():
            return rows_in.at[groups[k], halves[q], :, own]

        send(("twin", k, q), block, block, twin_sems, (k, q), twin)

    def pick(pair):
        return jnp.where(is_end, pair[0], pair[1])

    def gate(g, h):
        tile = min(units, 512)

        def columns_of(n, carry):
            at = pl.ds(pl.multiple_of(n * tile, tile), tile)
            block = rows_in[g, h, :, :, :width].reshape(hidden.shape[0], width)
            gated = jnp.dot(block, gate_up[0, :, at], preferred_element_type=f32)
            up = jnp.dot(block, gate_up[1, :, at], preferred_element_type=f32)
            hidden[:, at] = (gated / (1.0 + jnp.exp(-gated)) * up).astype(bf16)
            return carry

        lax.fori_loop(0, units // tile, columns_of, 0)

    def project(g, h):
        tile = 896 if width % 896 == 0 else 128
        more = rows_in[g, h, :, :, width:].reshape(hidden.shape[0], -1).astype(f32)
        column = lax.broadcasted_iota(jnp.int32, more.shape, 1)
        chosen = (
            (column == expert) | (column == expert + experts) | (column == expert + 2 * experts)
        )
        weight = jnp.sum(jnp.where(chosen, more, 0.0), axis=1, keepdims=True)

        def columns_of(n, carry):
            at = pl.ds(pl.multiple_of(n * tile, tile), tile)
            value = jnp.dot(hidden[...], down[:, at], preferred_element_type=f32)
            value = jnp.where(weight != 0.0, value * weight, 0.0).astype(bf16)
            parts[g, h, :, :, at] = value.reshape(2, 2 * rows, tile)
            return carry

        lax.fori_loop(0, width // tile, columns_of, 0)

    step = 32

    def accumulate(items):
        def one(i, carry):
            at = pl.multiple_of(i * step, step)
            for (g, yy, xx), start, size, buffer, index, offset in items:
                target = (
                    g, yy, xx,
                    pl.ds(pl.multiple_of(core * rows + at, step), step),
                    pl.ds(start, size),
                )
                source = index + (pl.ds(at, step), pl.ds(offset, size))
                total = parts[target].astype(f32) + buffer[source].astype(f32)
                parts[target] = total.astype(bf16)
            return carry

        lax.fori_loop(0, rows // step, one, 0)

    def to_core(k, q):
        send(
            ("core", k, q),
            lambda: parts.at[groups[k], halves[q], :, others],
            lambda: core_in.at[k, q],
            core_sems,
            (k, q),
            twin,
        )

    def core_add(k, q):
        arrive(("core", k, q))
        accumulate(
            [((groups[k], halves[q], i), 0, width, core_in, (k, q, i), 0) for i in range(2)]
        )

    def back_pair(name, k, t):
        g = groups[k]
        c = (0 if name == "a" else 2) + t
        sems = pair_sems if name == "a" else pair_b_sems
        index = (k, t) if name == "a" else (t,)

        def source():
            if t == 0:
                return parts.at[g, other_y, :, own, cols[c]]
            return parts.at[g, :, other_x, own, cols[c]]

        def target():
            ref = pair_in if name == "a" else pair_b
            return ref.at[index + (slice(None), slice(None), pl.ds(0, sizes[c]))]

        device = across_y if t == 0 else across_x
        send(("pair", name, k, t), source, target, sems, index, device)

    def back_last(name, k, t):
        g = groups[k]
        c = (0 if name == "a" else 2) + t
        sems = last_sems if name == "a" else last_b_sems
        index = (k, t) if name == "a" else (t,)
        arrive(("pair", name, k, t))
        buffer = pair_in if name == "a" else pair_b
        accumulate(
            [
                ((g, y, i) if t == 0 else (g, i, x), starts[c], sizes[c], buffer, index + (i,), 0)
                for i in range(2)
            ]
        )

        def source():
            if t == 0:
                return parts.at[g, y, other_x, own, cols[c]]
            return parts.at[g, other_y, x, own, cols[c]]

        def target():
            ref = last_in if name == "a" else last_b
            return ref.at[index + (slice(None), pl.ds(0, sizes[c]))]

        device = across_x if t == 0 else across_y
        send(("last", name, k, t), source, target, sems, index, device)

    def back_fin(name, k, t):
        c = (0 if name == "a" else 2) + t
        source = last_in if name == "a" else last_b
        index = (k, t) if name == "a" else (t,)
        arrive(("last", name, k, t))
        accumulate([((groups[k], y, x), starts[c], sizes[c], source, index, 0)])

    def inward(k):
        g = groups[k]
        falling = g < z
        source = jnp.where(falling, z + 1, z - 1)
        target = jnp.where(falling, z - 1, z + 1)
        valid = (source >= 0) & (source < planes)
        slot = jnp.where((target == g) & falling, planes, g)
        return g, valid, {"grp": jnp.clip(target, 0, planes - 1)}, slot

    inwards = [inward(k) for k in range(planes)]

    def back_a(k, t):
        g, valid, device, slot = inwards[k]

        @pl.when(valid)
        def _():
            block = chain_a.at[g, :, cols[t]]
            sem = back_a_sems.at
            mk(block, block, sem[0, k, t], sem[1, g, t], device).wait_recv()
            accumulate([((g, y, x), starts[t], sizes[t], chain_a, (g,), starts[t])])

        def copy():
            return mk(
                parts.at[g, y, x, own, cols[t]],
                chain_a.at[slot, :, cols[t]],
                back_a_sems.at[0, k, t],
                back_a_sems.at[1, slot, t],
                device,
            )

        copy().start()
        if ("ra", k, t) not in copies:
            copies["ra", k, t] = copy
            finals.append((None, copy))

    def back_b(k, c):
        g, valid, device, slot = inwards[k]
        yy, xx = quarters[c]

        @pl.when(valid)
        def _():
            block = chain_b.at[g, c]
            sem = back_b_sems.at
            mk(block, block, sem[0, k, c], sem[1, g, c], device).wait_recv()
            accumulate([((g, yy, xx), a_size, b_size, chain_b, (g, c), 0)])

        def copy():
            return mk(
                parts.at[g, yy, xx, own, b_cols],
                chain_b.at[slot, c],
                back_b_sems.at[0, k, c],
                back_b_sems.at[1, slot, c],
                device,
            )

        copy().start()
        if ("rb", k, c) not in copies:
            copies["rb", k, c] = copy
            finals.append((None, copy))

    def own_sides():
        return ((has_down, z, below), (has_up, planes, above))

    def own_b(c):
        for condition, slot, device in own_sides():

            @pl.when(condition)
            def _(slot=slot, device=device):
                block = chain_b.at[slot, c]
                sem = back_b_sems.at
                mk(block, block, sem[0, 0, c], sem[1, slot, c], device).wait_recv()
                accumulate([((z, *quarters[c]), a_size, b_size, chain_b, (slot, c), 0)])

    def own_a(t):
        for condition, slot, device in own_sides():

            @pl.when(condition)
            def _(slot=slot, device=device):
                block = chain_a.at[slot, :, pl.ds(starts[t], sizes[t])]
                sem = back_a_sems.at
                mk(block, block, sem[0, 0, t], sem[1, slot, t], device).wait_recv()
                accumulate([((z, y, x), starts[t], sizes[t], chain_a, (slot,), starts[t])])

    def scale_rows(ref, scale_of, count):
        size = ref.shape[0] // count

        def one(g, carry):
            at = pl.ds(pl.multiple_of(g * size, size), size)
            scale = jnp.where(is_hot, 1.0, scale_of(g))
            ref[at] = (ref[at].astype(f32) * scale).astype(bf16)
            return carry

        lax.fori_loop(0, count, one, 0)

    def scale_gate_up(j):
        loads[1 if j else 0].wait()
        scale_rows(
            gate_up.at[j],
            lambda g: gate_up_scale_ref[g, pl.ds(j, 1), :],
            gate_up_scale_ref.shape[0],
        )

    def scale_down():
        loads[2].wait()
        scale_rows(down, lambda g: down_scale_ref[pl.ds(g, 1), :], down_scale_ref.shape[0])

    came = [set(), set()]

    arrived = came[0]

    @pl.when(is_end)
    def _():
        spread("a", 0, 1, 0)
        spread("b", 0, 1, 0)
        out_a_own(1)
        spread("a", 0, 0, 0)
        spread("a", 0, 0, 1)
        spread("a", 0, 1, 1)
        out_a_own(0)
        out_a_hop(1, 0)
        spread("b", 0, 0, 1)
        spread("a", 0, 0, 2)
        spread("b", 0, 1, 1)
        out_b_own(0, 1)
        spread("b", 0, 0, 0)
        scale_down()
        spread("b", 0, 1, 2)
        spread("b", 0, 0, 2)
        to_twin(0, 0)
        out_a_hop(1, 1)
        out_a_hop(2, 0)
        spread("a", 2, 0, 0)
        out_b_own(1, 1)
        spread("a", 2, 0, 1)
        scale_gate_up(1)
        spread("a", 0, 1, 2)
        scale_gate_up(0)
        out_a_hop(2, 1)
        out_b_own(2, 1)
        arrive(("twin", 0, 0))

    arrived = came[1]

    @pl.when(is_mid)
    def _():
        out_a_own(0)
        spread("b", 0, 0, 0)
        spread("b", 0, 1, 0)
        out_a_own(1)
        spread("b", 0, 0, 2)
        spread("a", 0, 0, 0)
        scale_gate_up(0)
        scale_down()
        out_a_hop(1, 1)
        spread("a", 1, 1, 0)
        spread("a", 1, 1, 1)
        out_a_hop(2, 0)
        spread("a", 2, 0, 1)
        spread("b", 0, 0, 1)
        out_a_hop(2, 1)
        spread("b", 0, 1, 2)
        out_a_hop(1, 0)
        spread("a", 1, 0, 0)
        scale_gate_up(1)
        out_a_hop(3, 1)
        out_b_hop(1, 0)
        spread("a", 3, 1, 0)
        spread("a", 3, 1, 1)
        spread("a", 2, 1, 0)
        out_b_hop(1, 1)
        out_a_hop(3, 0)
        spread("a", 3, 0, 1)
        spread("a", 1, 0, 1)
        spread("a", 3, 0, 0)
        out_b_hop(1, 2)
        out_b_hop(3, 0)
        spread("b", 0, 1, 1)
        to_twin(1, 0)
        out_b_hop(3, 1)
        out_b_hop(1, 3)
        to_twin(3, 0)
        spread("a", 3, 0, 2)
        spread("a", 3, 1, 2)
        spread("a", 1, 1, 2)
        out_b_own(3, 1)
        out_b_hop(3, 2)
        arrive(("twin", 1, 0))

    at_group = pick((groups[0], groups[1]))
    at_half = pick((halves[0], halves[0]))
    gate(at_group, at_half)

    arrived = came[0]

    @pl.when(is_end)
    def _():
        out_a_hop(3, 1)
        out_b_own(3, 1)
        spread("a", 3, 1, 0)
        spread("a", 3, 1, 1)

    arrived = came[1]

    @pl.when(is_mid)
    def _():
        out_b_own(2, 1)
    project(at_group, at_half)

    arrived = came[0]

    @pl.when(is_end)
    def _():
        to_core(0, 0)
        spread("a", 2, 1, 0)
        out_a_hop(3, 0)
        spread("a", 3, 0, 0)
        to_twin(0, 1)
        spread("a", 3, 1, 2)
        spread("a", 3, 0, 1)
        arrive(("twin", 0, 1))

    arrived = came[1]

    @pl.when(is_mid)
    def _():
        to_core(1, 0)
        out_b_own(1, 1)
        out_b_hop(3, 3)
        spread("a", 2, 1, 1)
        spread("a", 0, 1, 0)
        spread("a", 2, 0, 0)
        out_b_own(0, 1)
        spread("a", 0, 1, 1)
        arrive(("twin", 3, 0))

    at_group = pick((groups[0], groups[3]))
    at_half = pick((halves[1], halves[0]))
    gate(at_group, at_half)

    arrived = came[0]

    @pl.when(is_end)
    def _():
        out_b_hop(3, 1)
        spread("a", 3, 0, 2)
        out_b_hop(3, 0)
        spread("a", 2, 0, 2)
        spread("a", 1, 1, 0)
        out_b_own(1, 0)
        to_twin(3, 0)
        spread("a", 2, 1, 2)
        spread("a", 1, 0, 0)

    arrived = came[1]

    @pl.when(is_mid)
    def _():
        spread("a", 1, 0, 2)
        to_twin(3, 1)
        out_b_hop(2, 3)
        out_b_hop(2, 2)
    project(at_group, at_half)

    arrived = came[0]

    @pl.when(is_end)
    def _():
        to_core(0, 1)
        spread("a", 2, 1, 1)
        out_b_hop(3, 2)
        arrive(("twin", 3, 0))

    arrived = came[1]

    @pl.when(is_mid)
    def _():
        to_core(3, 0)
        out_b_hop(2, 1)
        spread("a", 0, 0, 2)
        arrive(("twin", 3, 1))

    at_group = pick((groups[3], groups[3]))
    at_half = pick((halves[0], halves[1]))
    gate(at_group, at_half)

    arrived = came[0]

    @pl.when(is_end)
    def _():
        spread("a", 1, 1, 1)
        spread("a", 1, 0, 1)
        out_b_hop(3, 3)
        to_twin(3, 1)
        core_add(0, 0)

    arrived = came[1]

    @pl.when(is_mid)
    def _():
        to_twin(1, 1)
        core_add(3, 0)
        out_b_hop(2, 0)
        spread("a", 2, 0, 2)
        spread("a", 2, 1, 2)
        spread("a", 0, 1, 2)
        out_b_own(2, 0)
        out_b_own(3, 0)
    project(at_group, at_half)

    arrived = came[0]

    @pl.when(is_end)
    def _():
        to_core(3, 0)
        out_b_hop(2, 3)
        arrive(("twin", 3, 1))

    arrived = came[1]

    @pl.when(is_mid)
    def _():
        to_core(3, 1)
        spread("a", 0, 0, 1)
        arrive(("twin", 1, 1))

    at_group = pick((groups[3], groups[1]))
    at_half = pick((halves[1], halves[1]))
    gate(at_group, at_half)

    arrived = came[0]

    @pl.when(is_end)
    def _():
        out_b_hop(2, 2)
        out_b_own(2, 0)
        to_twin(2, 1)
        core_add(3, 0)
        back_b(3, 0)
        spread("a", 1, 0, 2)
        spread("a", 1, 1, 2)
        back_b(3, 1)

    arrived = came[1]

    @pl.when(is_mid)
    def _():
        core_add(3, 1)
        to_twin(2, 1)
    project(at_group, at_half)

    arrived = came[0]

    @pl.when(is_end)
    def _():
        to_core(3, 1)
        out_b_hop(2, 1)
        arrive(("twin", 2, 1))

    arrived = came[1]

    @pl.when(is_mid)
    def _():
        to_core(1, 1)
        out_b_own(1, 0)
        back_b(3, 1)
        core_add(1, 0)
        back_pair("a", 3, 0)
        back_pair("a", 3, 1)
        arrive(("twin", 2, 1))

    at_group = pick((groups[2], groups[2]))
    at_half = pick((halves[1], halves[1]))
    gate(at_group, at_half)

    arrived = came[0]

    @pl.when(is_end)
    def _():
        out_b_hop(2, 0)
        to_twin(2, 0)
        core_add(3, 1)
        back_pair("a", 3, 0)
        back_b(3, 2)
        back_pair("a", 3, 1)

    arrived = came[1]

    @pl.when(is_mid)
    def _():
        to_twin(2, 0)
        core_add(1, 1)
        out_b_own(0, 0)
        back_b(3, 0)
        back_pair("a", 1, 0)
    project(at_group, at_half)

    arrived = came[0]

    @pl.when(is_end)
    def _():
        to_core(2, 1)
        back_b(3, 3)
        arrive(("twin", 2, 0))

    arrived = came[1]

    @pl.when(is_mid)
    def _():
        to_core(2, 1)
        back_b(3, 2)
        back_pair("a", 1, 1)
        arrive(("twin", 2, 0))

    at_group = pick((groups[2], groups[2]))
    at_half = pick((halves[0], halves[0]))
    gate(at_group, at_half)

    arrived = came[0]

    @pl.when(is_end)
    def _():
        core_add(2, 1)
        back_b(2, 2)
        back_pair("a", 2, 0)

    arrived = came[1]

    @pl.when(is_mid)
    def _():
        to_twin(0, 1)
        back_last("a", 3, 0)
        core_add(2, 1)
        back_pair("a", 2, 0)
        to_twin(0, 0)
        back_b(1, 0)
        back_b(3, 3)
    project(at_group, at_half)

    arrived = came[0]

    @pl.when(is_end)
    def _():
        to_core(2, 0)
        out_b_hop(1, 3)
        back_last("a", 3, 0)
        back_b(2, 3)
        core_add(2, 0)
        out_b_own(0, 0)
        back_b(2, 0)
        back_pair("a", 2, 1)
        back_last("a", 3, 1)
        out_b_hop(1, 0)
        out_b_hop(1, 2)
        out_b_own(3, 0)
        to_twin(1, 1)
        core_add(0, 1)
        out_b_hop(1, 1)
        back_pair("a", 0, 0)
        back_fin("a", 3, 0)
        back_b(2, 1)
        back_pair("a", 0, 1)
        back_a(3, 0)
        to_twin(1, 0)
        arrive(("twin", 1, 1))

    arrived = came[1]

    @pl.when(is_mid)
    def _():
        to_core(2, 0)
        arrive(("twin", 0, 1))

    at_group = pick((groups[1], groups[0]))
    at_half = pick((halves[1], halves[1]))
    gate(at_group, at_half)

    arrived = came[1]

    @pl.when(is_mid)
    def _():
        back_b(1, 3)
        back_b(2, 3)
    project(at_group, at_half)

    arrived = came[0]

    @pl.when(is_end)
    def _():
        to_core(1, 1)
        back_fin("a", 3, 1)
        back_a(3, 1)
        arrive(("twin", 1, 0))

    arrived = came[1]

    @pl.when(is_mid)
    def _():
        to_core(0, 1)
        back_b(1, 2)
        core_add(2, 0)
        back_last("a", 1, 0)
        arrive(("twin", 0, 0))

    at_group = pick((groups[1], groups[0]))
    at_half = pick((halves[0], halves[0]))
    gate(at_group, at_half)

    arrived = came[0]

    @pl.when(is_end)
    def _():
        back_last("a", 2, 0)
        back_last("a", 2, 1)
        core_add(1, 1)
        back_b(1, 2)

    arrived = came[1]

    @pl.when(is_mid)
    def _():
        back_pair("a", 2, 1)
        back_last("a", 3, 1)
        back_b(2, 1)
        back_last("a", 2, 0)
        back_b(1, 1)
        back_fin("a", 3, 0)
        core_add(0, 1)
    project(at_group, at_half)

    arrived = came[0]

    @pl.when(is_end)
    def _():
        to_core(1, 0)
        own_b(2)
        back_b(1, 3)
        back_pair("a", 1, 0)
        core_add(1, 0)
        back_pair("a", 1, 1)
        own_b(1)
        back_b(1, 0)
        back_b(1, 1)
        back_fin("a", 2, 0)
        back_fin("a", 2, 1)
        own_b(0)
        own_b(3)
        back_a(2, 0)
        back_a(2, 1)
        back_pair("b", 0, 0)
        back_last("a", 1, 0)
        back_last("a", 1, 1)
        back_pair("b", 0, 1)
        back_fin("a", 1, 0)
        back_last("a", 0, 0)
        back_last("a", 0, 1)
        back_a(1, 0)
        back_fin("a", 1, 1)
        own_a(1)
        back_last("b", 0, 0)
        back_a(1, 1)
        back_last("b", 0, 1)
        own_a(0)
        back_fin("b", 0, 1)
        back_fin("a", 0, 0)
        back_fin("a", 0, 1)
        back_fin("b", 0, 0)

    arrived = came[1]

    @pl.when(is_mid)
    def _():
        to_core(0, 0)
        back_b(2, 2)
        back_b(2, 0)
        back_last("a", 1, 1)
        core_add(0, 0)
        back_fin("a", 3, 1)
        back_pair("a", 0, 1)
        back_pair("a", 0, 0)
        back_a(3, 1)
        back_fin("a", 1, 1)
        back_a(3, 0)
        back_fin("a", 1, 0)
        back_a(1, 1)
        own_b(1)
        own_b(2)
        back_last("a", 2, 1)
        own_b(3)
        own_b(0)
        back_pair("b", 0, 1)
        back_pair("b", 0, 0)
        back_last("a", 0, 0)
        back_fin("a", 2, 0)
        back_a(1, 0)
        back_a(2, 0)
        back_last("a", 0, 1)
        back_last("b", 0, 1)
        back_last("b", 0, 0)
        back_fin("a", 2, 1)
        back_a(2, 1)
        own_a(0)
        back_fin("b", 0, 0)
        back_fin("a", 0, 1)
        back_fin("b", 0, 1)
        back_fin("a", 0, 0)
        own_a(1)

    result = pltpu.make_async_copy(parts.at[z, y, x, own], out_ref, load_sem.at[4])
    result.start()
    for condition, copy in finals:
        if condition is None:
            copy().wait_send()
        else:

            @pl.when(condition)
            def _(copy=copy):
                copy().wait_send()
    result.wait()


def dense_shards(
    tokens, expert_ids, combine, hot_flags, gate_up_weight, gate_up_scale, down_weight, down_scale
):
    planes = lax.axis_size("grp")
    lane_count = lax.axis_size("ex")
    expert_count = planes // 2 * lane_count
    rows, width = tokens.shape
    units = down_weight.shape[2]
    extra = -(-3 * expert_count // 128) * 128
    starts, sizes = column_split(width)
    a_size, b_size = sizes[0] + sizes[1], sizes[2] + sizes[3]
    bf16 = jnp.bfloat16
    dma = pltpu.SemaphoreType.DMA
    return pl.pallas_call(
        functools.partial(fused_kernel, planes, expert_count),
        out_shape=jax.ShapeDtypeStruct((rows, width), bf16),
        in_specs=[pl.BlockSpec(memory_space=pl.ANY)] * 8,
        out_specs=pl.BlockSpec(memory_space=pl.ANY),
        scratch_shapes=[
            pltpu.VMEM((1, expert_count), jnp.int32),
            pltpu.VMEM(expert_ids.shape[::-1], jnp.int32),
            pltpu.VMEM(combine.shape[::-1], jnp.float32),
            pltpu.VMEM((gate_up_scale.shape[3], 2, units), jnp.float32),
            pltpu.VMEM(down_scale.shape[2:], jnp.float32),
            pltpu.VMEM((planes, 2, 2, 2 * rows, width + extra), bf16),
            pltpu.VMEM((planes, 2, 2, 2 * rows, width), bf16),
            pltpu.VMEM((planes, 2, 2, rows, width), bf16),
            pltpu.VMEM((planes, 2, 2, rows, max(sizes[:2])), bf16),
            pltpu.VMEM((planes, 2, rows, max(sizes[:2])), bf16),
            pltpu.VMEM((planes + 1, rows, a_size), bf16),
            pltpu.VMEM((planes + 1, 4, rows, b_size), bf16),
            pltpu.VMEM((2, 2, rows, max(sizes[2:])), bf16),
            pltpu.VMEM((2, rows, max(sizes[2:])), bf16),
            pltpu.VMEM((2, width, units), bf16),
            pltpu.VMEM((units, width), bf16),
            pltpu.VMEM((4 * rows, units), bf16),
            dma((10,)),
            dma((2, planes + 1, 2)),
            dma((2, planes + 1, 4)),
            dma((2, planes, 2, 3)),
            dma((2, 2, 3)),
            dma((2, planes, 2)),
            dma((2, planes, 2)),
            dma((2, planes, 2)),
            dma((2, planes, 2)),
            dma((2, planes + 1, 2)),
            dma((2, planes + 1, 4)),
            dma((2, 2)),
            dma((2, 2)),
        ],
        compiler_params=pltpu.CompilerParams(
            collective_id=0, has_side_effects=True, vmem_limit_bytes=67043328
        ),
    )(
        hot_flags.reshape(1, -1),
        tokens,
        expert_ids.T,
        combine.T,
        gate_up_weight[0, 0],
        jnp.transpose(gate_up_scale[0, 0], (1, 0, 2)),
        down_weight[0, 0],
        down_scale[0, 0],
    )


def shards(tokens, expert_ids, *rest):
    group_count = lax.axis_size("grp")
    lane_count = lax.axis_size("ex")
    token_count = tokens.shape[0]
    expert_count = group_count // 2 * lane_count
    route_count = token_count * expert_ids.shape[1]
    capacity = max(2, (5 * route_count + 4 * expert_count - 1) // (4 * expert_count))
    chip_rows = group_count * lane_count // 2 * token_count
    if group_count == 2 * 2 and lane_count == 2 * 2 * 2 and 2 * expert_count * capacity >= chip_rows:
        return dense_shards(tokens, expert_ids, *rest)
    return routed_shards(tokens, expert_ids, *rest)


def solution(mesh):
    return jax.shard_map(
        shards,
        mesh=mesh,
        in_specs=(
            P(("grp", "ex"), None),
            P(("grp", "ex"), None),
            P(("grp", "ex"), None),
            P(),
            P("grp", "ex", None, None, None),
            P("grp", "ex", None, None, None),
            P("grp", "ex", None, None),
            P("grp", "ex", None, None),
        ),
        out_specs=P(("grp", "ex"), None),
        check_vma=False,
    )
```
